512 devices in a mesh: ctx: 64 (over z, y), dp: 8 (over x, core).
Axes of the slice: x: 4, y: 4, z: 16, core: 2. Of those that a mesh axis runs over, the one named last changes fastest.
Arguments:
- q_in: bfloat16 [8, 8192, 2048], P('dp', 'ctx'), may hold values from -6 to 6
- k_in: bfloat16 [8, 8192, 2048], P('dp', 'ctx'), may hold values from -6 to 6
- v_in: bfloat16 [8, 8192, 2048], P('dp', 'ctx'), may hold values from -6 to 6
- grad_out: bfloat16 [8, 8192, 2048], P('dp', 'ctx'), may hold values from -6 to 6
- short_filter: float32 [3, 3, 2048], replicated, may hold values from -3.5 to 3.5
- residue: float32 [2048, 8], replicated, may hold values from -2 to 2
- rate: float32 [8], replicated, may hold values from 0.00012207031 to 0.1
Outputs:
- mixed: bfloat16 [8, 8192, 2048], P('dp', 'ctx')
- grad_q: bfloat16 [8, 8192, 2048], P('dp', 'ctx')
- grad_k: bfloat16 [8, 8192, 2048], P('dp', 'ctx')
- grad_v: bfloat16 [8, 8192, 2048], P('dp', 'ctx')
- grad_residue: float32 [2048, 8], P('ctx')
- grad_short: float32 [3, 3, 2048], replicated
The draws below stay inside these ranges and needn't reach their ends.
All inputs are finite; a program needn't handle non-finite values.
Results may differ from the reference program's by a relative error of at most 0.024.
Values may be sent and summed in bfloat16 or wider, within the bound.
A program may use at most 64 MiB of HBM per device.

```python
import math
import jax
import jax.numpy as jnp
from jax import lax

C = 2048
MODES = 8
SEQ = 8192
BATCH = 8


def block_levels(stream_key, dims, cuts, least, top_value):
    factor_of, own = 1.0, jax.random.fold_in(stream_key, 6)
    for position, blocks in cuts:
        draws = jnp.exp(jax.random.uniform(jax.random.fold_in(own, position), (blocks,), jnp.float32, least / len(cuts), top_value / len(cuts)))
        factor_of = factor_of * jnp.repeat(draws, dims[position] // blocks).reshape([-1 if axis == position else 1 for axis in range(len(dims))])
    return factor_of


def noise(key, dims, deviation, bound, shards=(), held_as=jnp.bfloat16):
    values = deviation * jax.random.normal(key, dims, jnp.float32)
    if shards:
        values = values * block_levels(key, dims, shards, -0.22, 0.18)
    return jnp.clip(values, -bound, bound).astype(held_as)


def setup_inputs(seed: int = 0) -> dict:
    seeds = jax.random.split(jax.random.key(seed), 8)
    return {
        "q_in": noise(seeds[0], (BATCH, SEQ, C), 1.0, 6.0, ((0, 8), (1, 64))),
        "k_in": noise(seeds[1], (BATCH, SEQ, C), 1.0, 6.0, ((0, 8), (1, 64))),
        "v_in": noise(seeds[2], (BATCH, SEQ, C), 1.0, 6.0, ((0, 8), (1, 64))),
        "grad_out": noise(seeds[3], (BATCH, SEQ, C), 1.0, 6.0, ((0, 8), (1, 64))),
        "short_filter": noise(seeds[4], (3, 3, C), 3 ** -0.5, 3.5, (), jnp.float32),
        "residue": noise(seeds[5], (C, MODES), MODES ** -0.5, 2.0, (), jnp.float32),
        "rate": jnp.clip(jnp.exp(jax.random.uniform(seeds[6], (MODES,), jnp.float32, math.log(0.00012207031), math.log(0.1))), 0.00012207031, 0.1),
    }


def shifted(values, lag_rows):
    if lag_rows == 0:
        return values
    length = values.shape[1]
    return jnp.pad(values, ((0, 0), (lag_rows, 0), (0, 0)))[:, :length, :]

def ahead(values, lead_rows):
    if lead_rows == 0:
        return values
    return jnp.pad(values, ((0, 0), (0, lead_rows), (0, 0)))[:, lead_rows:, :]

def reference(q_in, k_in, v_in, grad_out, short_filter, residue, rate):
    inputs = [q_in.astype(jnp.float32), k_in.astype(jnp.float32), v_in.astype(jnp.float32)]
    shorts = []
    for branch in range(3):
        total = short_filter[branch, 0][None, None, :] * inputs[branch]
        for tap_at in range(1, 3):
            total = total + short_filter[branch, tap_at][None, None, :] * shifted(inputs[branch], tap_at)
        shorts.append(total)
    query, keyed, valued = shorts
    gated = (keyed * valued).astype(jnp.bfloat16)
    d_conv = (grad_out.astype(jnp.float32) * query).astype(jnp.bfloat16)
    decay = jnp.exp(-rate)
    gains = jnp.sqrt(1.0 - jnp.exp(-2.0 * rate))
    columns = (residue * gains[None, :]).T
    source = jnp.transpose(gated.astype(jnp.float32), (1, 0, 2))
    cotangent = jnp.transpose(d_conv.astype(jnp.float32), (1, 0, 2))
    batch = q_in.shape[0]
    width = q_in.shape[2]
    modes = rate.shape[0]

    def forward(carry, item):
        state, accum = carry
        x_row, d_row = item
        state = decay[None, :, None] * state + x_row[:, None, :]
        out_row = lax.optimization_barrier(jnp.sum(columns[None] * state, axis=1))
        accum = accum + lax.optimization_barrier(jnp.sum(d_row[:, None, :] * state, axis=0))
        return ((state, accum), out_row)
    start = jnp.zeros((batch, modes, width), jnp.float32)
    (unused_state, accum), conv_rows = lax.scan(forward, (start, jnp.zeros((modes, width), jnp.float32)), (source, cotangent))

    def backward(state, d_row):
        state = decay[None, :, None] * state + d_row[:, None, :]
        return (state, lax.optimization_barrier(jnp.sum(columns[None] * state, axis=1)))
    unused_back, back_rows = lax.scan(backward, start, cotangent, reverse=True)
    conv = jnp.transpose(conv_rows, (1, 0, 2)).astype(jnp.bfloat16)
    d_gated = jnp.transpose(back_rows, (1, 0, 2)).astype(jnp.bfloat16)
    grad_residue = (gains[:, None] * accum).T
    conv_f = conv.astype(jnp.float32)
    mixed = (query * conv_f).astype(jnp.bfloat16)
    gated_back = d_gated.astype(jnp.float32)
    d_shorts = [grad_out.astype(jnp.float32) * conv_f, gated_back * valued, gated_back * keyed]
    grads = []
    short_rows = []
    for branch in range(3):
        total = short_filter[branch, 0][None, None, :] * d_shorts[branch]
        for tap_at in range(1, 3):
            total = total + short_filter[branch, tap_at][None, None, :] * ahead(d_shorts[branch], tap_at)
        grads.append(total.astype(jnp.bfloat16))
        short_rows.append(jnp.stack([lax.optimization_barrier(jnp.sum(d_shorts[branch] * shifted(inputs[branch], tap_at), axis=(0, 1))) for tap_at in range(3)]))
    return (mixed, grads[0], grads[1], grads[2], grad_residue, jnp.stack(short_rows))
```

```python
import functools

import jax
import jax.numpy as jnp
from jax import lax
from jax.experimental import pallas as pl
from jax.experimental.pallas import tpu as pltpu
from jax.sharding import PartitionSpec as P

MESH = pl.DeviceIdType.MESH
ROWS = 128
CHANNELS = 2048
MODES = 8
LANES = 128
BLOCKS = CHANNELS // LANES
WIDE = 256
NZ = 16
NY = 4
NDP = 8
PLANE = NY * NDP
QUARTER = CHANNELS // NY
F32 = jnp.float32
BF16 = jnp.bfloat16


def split_bf16(value):
    high = value.astype(BF16).astype(F32)
    return high, value - high


def two_row_tile(first, second, at):
    width = first.shape[1]
    row = lax.broadcasted_iota(jnp.int32, (8, width), 0)
    return jnp.where(row == at, first, jnp.where(row == at + 1, second, 0.0))


def rate_rows(rate_ref, width):
    row = lax.broadcasted_iota(jnp.int32, (MODES, width), 0)
    total = jnp.zeros((MODES, width), F32)
    for mode in range(MODES):
        total = jnp.where(row == mode, rate_ref[mode], total)
    return total


def plane_peer(index):
    return index // NDP, lax.rem(index, NDP)


def operator_kernel(
    rate_ref,
    q_ref,
    k_ref,
    v_ref,
    go_ref,
    before_ref,
    after_ref,
    filter_ref,
    residue_ref,
    mixed_ref,
    gq_ref,
    gk_ref,
    gv_ref,
    gres_ref,
    gshort_ref,
    short_q,
    short_k,
    short_v,
    gated,
    d_conv,
    tail_gd,
    fwd_table,
    bwd_table,
    modal,
    conv_local,
    back_local,
    res_local,
    ends,
    y_send,
    y_recv,
    z_send,
    z_recv,
    b_send,
    b_recv,
    enter,
    edge,
    r_send,
    r_recv,
    p_send,
    p_recv,
    a_recv,
    turned,
    send_sems,
    recv_sems,
):
    ctx = lax.axis_index("ctx")
    dp = lax.axis_index("dp")
    z = ctx // NY
    y = lax.rem(ctx, NY)
    plane = y * NDP + dp

    barrier = pltpu.get_barrier_semaphore()

    def greet_line(step, carry):
        peer = lax.rem(z + step, NZ)
        pl.semaphore_signal(
            barrier, inc=1, device_id={"ctx": peer * NY + y}, device_id_type=MESH
        )
        return carry

    def greet_plane(step, carry):
        peer_y, peer_dp = plane_peer(lax.rem(plane + step, PLANE))
        pl.semaphore_signal(
            barrier,
            inc=1,
            device_id={"ctx": z * NY + peer_y, "dp": peer_dp},
            device_id_type=MESH,
        )
        return carry

    lax.fori_loop(1, NZ, greet_line, 0)
    lax.fori_loop(1, PLANE, greet_plane, 0)

    def taps(branch, lanes):
        return [filter_ref[branch, j : j + 1, lanes] for j in range(3)]

    def before_tile(branch, lanes):
        rows = before_ref[branch, :, lanes].astype(F32)
        return two_row_tile(rows[0:1], rows[1:2], 6)

    def after_tile(branch, lanes):
        rows = after_ref[branch, :, lanes].astype(F32)
        return two_row_tile(rows[0:1], rows[1:2], 0)

    inputs = (q_ref, k_ref, v_ref)
    shorts = (short_q, short_k, short_v)

    def short_step(block, carry):
        lanes = pl.ds(pl.multiple_of(block * LANES, LANES), LANES)
        results = []
        for branch in range(3):
            values = inputs[branch][:, lanes].astype(F32)
            extended = jnp.concatenate(
                [before_tile(branch, lanes), values, after_tile(branch, lanes)], axis=0
            )
            first, second, third = taps(branch, lanes)
            total = (
                first * extended[8:]
                + second * pltpu.roll(extended, 1, 0)[8:]
                + third * pltpu.roll(extended, 2, 0)[8:]
            )
            shorts[branch][:, lanes] = total
            results.append(total)
        query, keyed, valued = results
        cot = jnp.concatenate([go_ref[:, lanes].astype(F32), after_tile(3, lanes)], axis=0)
        gate = (keyed * valued).astype(BF16)
        d_out = (cot * query).astype(BF16)
        gated[:, lanes] = gate[:ROWS]
        d_conv[:, lanes] = d_out[:ROWS]
        tail_gd[0:8, lanes] = (keyed[ROWS:] * valued[ROWS:]).astype(BF16).astype(F32)
        tail_gd[8:16, lanes] = (cot[ROWS:] * query[ROWS:]).astype(BF16).astype(F32)
        return carry

    lax.fori_loop(0, BLOCKS, short_step, 0)

    rates = rate_rows(rate_ref, ROWS)
    place = lax.broadcasted_iota(jnp.int32, (MODES, ROWS), 1).astype(F32)
    for slot, offsets, operand in ((0, ROWS - 1.0 - place, gated), (1, place, d_conv)):
        high, low = split_bf16(jnp.exp(-rates * offsets))
        table = jnp.concatenate([high, low], axis=0).astype(BF16)
        product = jnp.dot(table, operand[...], preferred_element_type=F32)
        ends[slot * 8 : slot * 8 + 8, :] = product[:8] + product[8:]

    for part in range(NY):
        y_send[part] = ends[:, part * QUARTER : (part + 1) * QUARTER]

    pl.semaphore_wait(barrier, NZ - 1 + PLANE - 1)

    def y_copy(source, target, step, slot):
        peer = lax.rem(y + step, NY)
        return pltpu.make_async_remote_copy(
            src_ref=source.at[peer],
            dst_ref=target.at[y],
            send_sem=send_sems.at[slot],
            recv_sem=recv_sems.at[slot],
            device_id={"ctx": z * NY + peer},
            device_id_type=MESH,
        )

    def settle(source, target, count, slot):
        done = pltpu.make_async_remote_copy(
            src_ref=source.at[pl.ds(0, count)],
            dst_ref=target.at[pl.ds(0, count)],
            send_sem=send_sems.at[slot],
            recv_sem=recv_sems.at[slot],
            device_id={"ctx": z * NY + lax.rem(y + 1, NY)},
            device_id_type=MESH,
        )
        done.wait_send()
        done.wait_recv()

    for step in range(1, NY):
        y_copy(y_send, y_recv, step, 0).start()
    y_recv[y] = y_send[y]

    row_at = lax.broadcasted_iota(jnp.int32, (ROWS, ROWS), 0)
    col_at = lax.broadcasted_iota(jnp.int32, (ROWS, ROWS), 1)
    for mode in range(MODES):
        speed = rate_ref[mode]
        here = slice(mode * ROWS, (mode + 1) * ROWS)
        for table, lag in ((fwd_table, row_at - col_at), (bwd_table, col_at - row_at)):
            power = jnp.exp(-speed * jnp.maximum(lag, 0).astype(F32))
            high, low = split_bf16(jnp.where(lag >= 0, power, 0.0))
            table[here, 0:ROWS] = high.astype(BF16)
            table[here, ROWS : 2 * ROWS] = low.astype(BF16)

    settle(y_send, y_recv, NY - 1, 0)

    speeds = rate_rows(rate_ref, QUARTER)
    step_decay = jnp.exp(-speeds * float(ROWS))
    group_decay = jnp.exp(-speeds * float(ROWS * NY))

    def fold(value):
        return jnp.concatenate([value[:, : QUARTER // 2], value[:, QUARTER // 2 :]], axis=0)

    def unfold(value):
        return jnp.concatenate([value[:8], value[8:]], axis=1)

    ahead_total = y_recv[0, 0:8]
    back_total = y_recv[NY - 1, 8:16]
    for index in range(1, NY):
        ahead_total = ahead_total * step_decay + y_recv[index, 0:8]
        back_total = back_total * step_decay + y_recv[NY - 1 - index, 8:16]
    z_send[0] = fold(ahead_total).astype(BF16)
    z_send[1] = fold(back_total).astype(BF16)

    def z_start(step, carry):
        peer = lax.rem(z + step, NZ)
        pltpu.make_async_remote_copy(
            src_ref=z_send.at[jnp.where(peer < z, 1, 0)],
            dst_ref=z_recv.at[z],
            send_sem=send_sems.at[1],
            recv_sem=recv_sems.at[1],
            device_id={"ctx": peer * NY + y},
            device_id_type=MESH,
        ).start()
        return carry

    lax.fori_loop(1, NZ, z_start, 0)
    z_recv[z] = jnp.zeros((16, QUARTER // 2), BF16)

    gain_rows = jnp.sqrt(1.0 - jnp.exp(-2.0 * rate_rows(rate_ref, WIDE)))

    def modal_step(block, carry):
        lanes = pl.ds(pl.multiple_of(block * WIDE, WIDE), WIDE)
        columns = residue_ref[:, lanes] * gain_rows
        source = gated[:, lanes]
        modal[...] = jnp.dot(
            fwd_table[...],
            jnp.concatenate([source, source], axis=0),
            preferred_element_type=F32,
        )
        cot = d_conv[:, lanes].astype(F32)
        total = jnp.zeros((ROWS, WIDE), F32)
        for mode in range(MODES):
            state = modal[mode * ROWS : (mode + 1) * ROWS, :]
            total = total + columns[mode : mode + 1] * state
            res_local[mode : mode + 1, lanes] = jnp.sum(cot * state, axis=0, keepdims=True)
        conv_local[:, lanes] = total
        source = d_conv[:, lanes]
        modal[...] = jnp.dot(
            bwd_table[...],
            jnp.concatenate([source, source], axis=0),
            preferred_element_type=F32,
        )
        total = jnp.zeros((ROWS, WIDE), F32)
        for mode in range(MODES):
            total = total + columns[mode : mode + 1] * modal[mode * ROWS : (mode + 1) * ROWS, :]
        back_local[:, lanes] = total
        return carry

    lax.fori_loop(0, CHANNELS // WIDE, modal_step, 0)

    done = pltpu.make_async_remote_copy(
        src_ref=z_recv.at[pl.ds(0, NZ - 1)],
        dst_ref=z_recv.at[pl.ds(0, NZ - 1)],
        send_sem=send_sems.at[1],
        recv_sem=recv_sems.at[1],
        device_id={"ctx": lax.rem(z + 1, NZ) * NY + y},
        device_id_type=MESH,
    )
    done.wait_send()
    done.wait_recv()

    start = jnp.zeros((MODES, QUARTER), F32)
    finish = jnp.zeros((MODES, QUARTER), F32)
    for index in range(NZ):
        start = jnp.where(
            index < z, start * group_decay + unfold(z_recv[index].astype(F32)), start
        )
        other = NZ - 1 - index
        finish = jnp.where(
            other > z, finish * group_decay + unfold(z_recv[other].astype(F32)), finish
        )
    for index in range(NY):
        b_send[index, 0:8] = start
        start = start * step_decay + y_recv[index, 0:8]
        other = NY - 1 - index
        b_send[other, 8:16] = finish
        finish = finish * step_decay + y_recv[other, 8:16]

    for step in range(1, NY):
        y_copy(b_send, b_recv, step, 2).start()
    b_recv[y] = b_send[y]
    settle(b_send, b_recv, NY - 1, 2)

    wide_speeds = rate_rows(rate_ref, QUARTER)
    one = jnp.exp(-wide_speeds)
    gains = jnp.sqrt(1.0 - jnp.exp(-2.0 * wide_speeds))
    for part in range(NY):
        lanes = slice(part * QUARTER, (part + 1) * QUARTER)
        columns = residue_ref[:, lanes] * gains
        state = b_recv[part, 0:8]
        costate = b_recv[part, 8:16]
        for slot, value in ((0, columns * state), (1, columns * costate)):
            high, low = split_bf16(value)
            enter[slot, :, lanes] = jnp.concatenate([high, low, high, low], axis=0).astype(BF16)
        out_state = state * step_decay + ends[0:8, lanes]
        next_first = one * out_state + tail_gd[0:1, lanes]
        next_second = one * next_first + tail_gd[1:2, lanes]
        back_second = (costate - tail_gd[8:9, lanes]) / one
        edge[0:8, lanes] = two_row_tile(
            jnp.sum(columns * next_first, axis=0, keepdims=True),
            jnp.sum(columns * next_second, axis=0, keepdims=True),
            0,
        )
        edge[8:16, lanes] = two_row_tile(
            jnp.sum(columns * costate, axis=0, keepdims=True),
            jnp.sum(columns * back_second, axis=0, keepdims=True),
            0,
        )
        total = gains * (res_local[:, lanes] + state * one * ends[8:16, lanes])
        for offset in range(QUARTER // LANES):
            block = part * (QUARTER // LANES) + offset
            r_send[2 * block + 1, 0:8] = total[:, offset * LANES : (offset + 1) * LANES]
            r_send[2 * block + 1, 8:9] = jnp.zeros((1, LANES), F32)

    lane_at = lax.broadcasted_iota(jnp.int32, (ROWS, 4 * MODES), 1)
    lane_rate = jnp.zeros((ROWS, 4 * MODES), F32)
    for mode in range(MODES):
        lane_rate = jnp.where(lax.rem(lane_at, MODES) == mode, rate_ref[mode], lane_rate)
    place = lax.broadcasted_iota(jnp.int32, (ROWS, 4 * MODES), 0).astype(F32)

    def spread(offsets):
        high, low = split_bf16(jnp.exp(-lane_rate * offsets))
        return jnp.where(lane_at < 2 * MODES, high, low).astype(BF16)

    spread_fwd = spread(place + 1.0)
    spread_back = spread(ROWS - place)
    outs = (gq_ref, gk_ref, gv_ref)

    def final_step(block, carry):
        lanes = pl.ds(pl.multiple_of(block * LANES, LANES), LANES)
        conv = conv_local[:, lanes] + jnp.dot(
            spread_fwd, enter[0, :, lanes], preferred_element_type=F32
        )
        back = back_local[:, lanes] + jnp.dot(
            spread_back, enter[1, :, lanes], preferred_element_type=F32
        )
        conv_ext = jnp.concatenate([conv, edge[0:8, lanes]], axis=0)
        back_ext = jnp.concatenate([back, edge[8:16, lanes]], axis=0)
        cot = jnp.concatenate([go_ref[:, lanes].astype(F32), after_tile(3, lanes)], axis=0)
        mixed_ref[:, lanes] = (short_q[0:ROWS, lanes] * conv).astype(BF16)
        d_shorts = (cot * conv_ext, back_ext * short_v[:, lanes], back_ext * short_k[:, lanes])
        for branch in range(3):
            value = d_shorts[branch]
            first, second, third = taps(branch, lanes)
            total = (
                first * value[:ROWS]
                + second * pltpu.roll(value, ROWS + 8 - 1, 0)[:ROWS]
                + third * pltpu.roll(value, ROWS + 8 - 2, 0)[:ROWS]
            )
            outs[branch][:, lanes] = total.astype(BF16)
            extended = jnp.concatenate(
                [before_tile(branch, lanes), inputs[branch][:, lanes].astype(F32)], axis=0
            )
            for tap_at in range(3):
                moved = pltpu.roll(extended, tap_at, 0)[8:] if tap_at else extended[8:]
                at = branch * 3 + tap_at
                r_send[2 * block, at : at + 1] = jnp.sum(
                    value[:ROWS] * moved, axis=0, keepdims=True
                )
        return carry

    lax.fori_loop(0, BLOCKS, final_step, 0)

    def plane_start(source_of, target, slot):
        def start_one(step, carry):
            peer = lax.rem(plane + step, PLANE)
            peer_y, peer_dp = plane_peer(peer)
            pltpu.make_async_remote_copy(
                src_ref=source_of(peer),
                dst_ref=target.at[plane],
                send_sem=send_sems.at[slot],
                recv_sem=recv_sems.at[slot],
                device_id={"ctx": z * NY + peer_y, "dp": peer_dp},
                device_id_type=MESH,
            ).start()
            return carry

        lax.fori_loop(1, PLANE, start_one, 0)

    plane_start(lambda peer: r_send.at[peer], r_recv, 3)
    r_recv[plane] = r_send[plane]
    settle(r_send, r_recv, PLANE - 1, 3)
    total = r_recv[0]
    for index in range(1, PLANE):
        total = total + r_recv[index]
    p_send[...] = total

    def line_start(step, carry):
        peer = lax.rem(z + step, NZ)
        pltpu.make_async_remote_copy(
            src_ref=p_send,
            dst_ref=p_recv.at[z],
            send_sem=send_sems.at[4],
            recv_sem=recv_sems.at[4],
            device_id={"ctx": peer * NY + y},
            device_id_type=MESH,
        ).start()
        return carry

    lax.fori_loop(1, NZ, line_start, 0)
    p_recv[z] = p_send[...]
    settle(p_recv, p_recv, NZ - 1, 4)
    total = p_recv[0]
    for index in range(1, NZ):
        total = total + p_recv[index]
    a_recv[plane] = total
    plane_start(lambda peer: a_recv.at[plane], a_recv, 5)
    settle(a_recv, a_recv, PLANE - 1, 5)
    for block in range(BLOCKS):
        gshort_ref[:, block * LANES : (block + 1) * LANES] = a_recv[2 * block]
    mine = a_recv[2 * z + 1][0:8]
    turned[...] = mine.T
    gres_ref[...] = turned[pl.ds(pl.multiple_of(y * 32, 32), 32), :]


def shards(q_in, k_in, v_in, grad_out, short_filter, residue, rate):
    inputs = (q_in[0], k_in[0], v_in[0], grad_out[0])
    count = lax.axis_size("ctx")
    tails = jnp.stack([item[ROWS - 2 :] for item in inputs[:3]])
    heads = jnp.stack([item[:2] for item in inputs])
    before = lax.ppermute(tails, "ctx", [(i, i + 1) for i in range(count - 1)])
    after = lax.ppermute(heads, "ctx", [(i + 1, i) for i in range(count - 1)])
    vmem = pl.BlockSpec(memory_space=pltpu.VMEM)
    smem = pl.BlockSpec(memory_space=pltpu.SMEM)
    block = jax.ShapeDtypeStruct((ROWS, CHANNELS), BF16)
    mixed, gq, gk, gv, gres, gshort = pl.pallas_call(
        operator_kernel,
        out_shape=(
            block,
            block,
            block,
            block,
            jax.ShapeDtypeStruct((CHANNELS // 64, MODES), F32),
            jax.ShapeDtypeStruct((9, CHANNELS), F32),
        ),
        in_specs=[smem] + [vmem] * 8,
        out_specs=(vmem,) * 6,
        scratch_shapes=[
            pltpu.VMEM((ROWS + 8, CHANNELS), F32),
            pltpu.VMEM((ROWS + 8, CHANNELS), F32),
            pltpu.VMEM((ROWS + 8, CHANNELS), F32),
            pltpu.VMEM((ROWS, CHANNELS), BF16),
            pltpu.VMEM((ROWS, CHANNELS), BF16),
            pltpu.VMEM((16, CHANNELS), F32),
            pltpu.VMEM((MODES * ROWS, 2 * ROWS), BF16),
            pltpu.VMEM((MODES * ROWS, 2 * ROWS), BF16),
            pltpu.VMEM((MODES * ROWS, WIDE), F32),
            pltpu.VMEM((ROWS, CHANNELS), F32),
            pltpu.VMEM((ROWS, CHANNELS), F32),
            pltpu.VMEM((MODES, CHANNELS), F32),
            pltpu.VMEM((16, CHANNELS), F32),
            pltpu.VMEM((NY, 16, QUARTER), F32),
            pltpu.VMEM((NY, 16, QUARTER), F32),
            pltpu.VMEM((2, 16, QUARTER // 2), BF16),
            pltpu.VMEM((NZ, 16, QUARTER // 2), BF16),
            pltpu.VMEM((NY, 16, QUARTER), F32),
            pltpu.VMEM((NY, 16, QUARTER), F32),
            pltpu.VMEM((2, 4 * MODES, CHANNELS), BF16),
            pltpu.VMEM((16, CHANNELS), F32),
            pltpu.VMEM((PLANE, 9, LANES), F32),
            pltpu.VMEM((PLANE, 9, LANES), F32),
            pltpu.VMEM((9, LANES), F32),
            pltpu.VMEM((NZ, 9, LANES), F32),
            pltpu.VMEM((PLANE, 9, LANES), F32),
            pltpu.VMEM((LANES, MODES), F32),
            pltpu.SemaphoreType.DMA((6,)),
            pltpu.SemaphoreType.DMA((6,)),
        ],
        name="operator",
        compiler_params=pltpu.CompilerParams(
            collective_id=0, has_side_effects=True, vmem_limit_bytes=48 << 20
        ),
    )(rate, *inputs, before, after, short_filter, residue.T)
    return (
        mixed[None],
        gq[None],
        gk[None],
        gv[None],
        gres,
        gshort.reshape(3, 3, CHANNELS),
    )


def solution(mesh):
    placed = P("dp", "ctx", None)
    return jax.shard_map(
        shards,
        mesh=mesh,
        in_specs=(placed, placed, placed, placed, P(), P(), P()),
        out_specs=(placed, placed, placed, placed, P("ctx", None), P()),
        check_vma=False,
    )
```

```python
import functools

import jax
import jax.numpy as jnp
from jax import lax
from jax.experimental import pallas as pl
from jax.experimental.pallas import tpu as pltpu
from jax.sharding import PartitionSpec as P

MESH = pl.DeviceIdType.MESH
ROWS = 128
CHANNELS = 2048
MODES = 8
LANES = 128
BLOCKS = CHANNELS // LANES
WIDE = 256
NZ = 16
NY = 4
NDP = 8
PLANE = NY * NDP
QUARTER = CHANNELS // NY
GRANT = 56 << 20
F32 = jnp.float32
BF16 = jnp.bfloat16


def split_bf16(value):
    high = value.astype(BF16).astype(F32)
    return high, value - high


def two_row_tile(first, second, at):
    width = first.shape[1]
    row = lax.broadcasted_iota(jnp.int32, (8, width), 0)
    return jnp.where(row == at, first, jnp.where(row == at + 1, second, 0.0))


def rate_rows(rate_ref, width):
    row = lax.broadcasted_iota(jnp.int32, (MODES, width), 0)
    total = jnp.zeros((MODES, width), F32)
    for mode in range(MODES):
        total = jnp.where(row == mode, rate_ref[mode], total)
    return total


def plane_peer(index):
    return index // NDP, lax.rem(index, NDP)


def operator_kernel(
    rate_ref,
    q_hbm,
    k_hbm,
    v_hbm,
    go_hbm,
    filter_ref,
    residue_ref,
    mixed_hbm,
    gq_hbm,
    gk_hbm,
    gv_hbm,
    gres_ref,
    gshort_ref,
    mixed_ref,
    gq_ref,
    gk_ref,
    gv_ref,
    q_ref,
    k_ref,
    v_ref,
    go_ref,
    tail_send,
    head_send,
    tail_recv,
    head_recv,
    short_q,
    short_k,
    short_v,
    gated,
    d_conv,
    tail_gd,
    fwd_table,
    bwd_table,
    modal,
    conv_local,
    back_local,
    res_local,
    ends,
    y_send,
    y_recv,
    z_send,
    z_recv,
    b_send,
    b_recv,
    enter,
    edge,
    m_send,
    m_recv,
    l_send,
    l_recv,
    r_send,
    r_recv,
    p_send,
    p_recv,
    short_sum,
    res_sum,
    load_sems,
    store_sems,
    send_sems,
    recv_sems,
):
    ctx = lax.axis_index("ctx")
    dp = lax.axis_index("dp")
    z = ctx // NY
    y = lax.rem(ctx, NY)
    plane = y * NDP + dp

    inputs = (q_ref, k_ref, v_ref, go_ref)
    loads = [
        pltpu.make_async_copy(source, target, load_sems.at[index])
        for index, (source, target) in enumerate(zip((q_hbm, k_hbm, v_hbm, go_hbm), inputs))
    ]
    for load in loads:
        load.start()

    barrier = pltpu.get_barrier_semaphore()
    count = NZ * NY
    following = lax.rem(ctx + 1, count)
    preceding = lax.rem(ctx + count - 1, count)
    for neighbour in (following, preceding):
        pl.semaphore_signal(
            barrier, inc=1, device_id={"ctx": neighbour}, device_id_type=MESH
        )

    def greet_line(step, carry):
        peer = lax.rem(z + step, NZ)
        pl.semaphore_signal(
            barrier, inc=1, device_id={"ctx": peer * NY + y}, device_id_type=MESH
        )
        return carry

    def greet_plane(step, carry):
        peer_y, peer_dp = plane_peer(lax.rem(plane + step, PLANE))
        pl.semaphore_signal(
            barrier,
            inc=1,
            device_id={"ctx": z * NY + peer_y, "dp": peer_dp},
            device_id_type=MESH,
        )
        return carry

    lax.fori_loop(1, NZ, greet_line, 0)
    lax.fori_loop(1, PLANE, greet_plane, 0)

    def taps(branch, lanes):
        return [filter_ref[branch, j : j + 1, lanes] for j in range(3)]

    for load in loads:
        load.wait()

    row_eight = lax.broadcasted_iota(jnp.int32, (8, CHANNELS), 0)
    tails = jnp.zeros((8, CHANNELS), F32)
    heads = jnp.zeros((8, CHANNELS), F32)
    for branch in range(4):
        last = inputs[branch][ROWS - 16 : ROWS, :].astype(F32)
        first = inputs[branch][0:16, :].astype(F32)
        for index in range(2):
            here = row_eight == 2 * branch + index
            heads = jnp.where(here, first[index : index + 1], heads)
            if branch < 3:
                tails = jnp.where(here, last[14 + index : 15 + index], tails)
    tail_send[...] = tails.astype(BF16)
    head_send[...] = heads.astype(BF16)

    pl.semaphore_wait(barrier, NZ - 1 + PLANE - 1 + 2)
    halos = [
        pltpu.make_async_remote_copy(
            src_ref=source,
            dst_ref=target,
            send_sem=send_sems.at[slot],
            recv_sem=recv_sems.at[slot],
            device_id={"ctx": neighbour},
            device_id_type=MESH,
        )
        for slot, source, target, neighbour in (
            (6, tail_send, tail_recv, following),
            (7, head_send, head_recv, preceding),
        )
    ]
    for halo in halos:
        halo.start()

    def before_tile(branch, lanes):
        rows = tail_recv[:, lanes].astype(F32)[2 * branch : 2 * branch + 2]
        tile = two_row_tile(rows[0:1], rows[1:2], 6)
        return jnp.where(ctx == 0, 0.0, tile)

    def after_tile(branch, lanes):
        rows = head_recv[:, lanes].astype(F32)[2 * branch : 2 * branch + 2]
        tile = two_row_tile(rows[0:1], rows[1:2], 0)
        return jnp.where(ctx == count - 1, 0.0, tile)

    shorts = (short_q, short_k, short_v)

    def convolve(branch, lanes, extended):
        first, second, third = taps(branch, lanes)
        return (
            first * extended[8:]
            + second * pltpu.roll(extended, 1, 0)[8:]
            + third * pltpu.roll(extended, 2, 0)[8:]
        )

    def short_step(block, carry):
        lanes = pl.ds(pl.multiple_of(block * LANES, LANES), LANES)
        results = []
        for branch in range(3):
            values = inputs[branch][:, lanes].astype(F32)
            extended = jnp.concatenate([jnp.zeros((8, LANES), F32), values], axis=0)
            total = convolve(branch, lanes, extended)
            shorts[branch][0:ROWS, lanes] = total
            results.append(total)
        query, keyed, valued = results
        gated[:, lanes] = (keyed * valued).astype(BF16)
        d_conv[:, lanes] = (go_ref[:, lanes].astype(F32) * query).astype(BF16)
        return carry

    lax.fori_loop(0, BLOCKS, short_step, 0)

    for halo in halos:
        halo.wait_recv()

    def patch_step(block, carry):
        lanes = pl.ds(pl.multiple_of(block * LANES, LANES), LANES)
        firsts = []
        nexts = []
        for branch in range(3):
            values = inputs[branch][0:16, lanes].astype(F32)
            extended = jnp.concatenate([before_tile(branch, lanes), values], axis=0)
            firsts.append(convolve(branch, lanes, extended))
            shorts[branch][0:16, lanes] = firsts[branch]
            values = inputs[branch][ROWS - 16 : ROWS, lanes].astype(F32)[8:]
            extended = jnp.concatenate([values, after_tile(branch, lanes)], axis=0)
            nexts.append(convolve(branch, lanes, extended))
            shorts[branch][ROWS : ROWS + 8, lanes] = nexts[branch]
        gated[0:16, lanes] = (firsts[1] * firsts[2]).astype(BF16)
        d_conv[0:16, lanes] = (go_ref[0:16, lanes].astype(F32) * firsts[0]).astype(BF16)
        tail_gd[0:8, lanes] = (nexts[1] * nexts[2]).astype(BF16).astype(F32)
        tail_gd[8:16, lanes] = (after_tile(3, lanes) * nexts[0]).astype(BF16).astype(F32)
        return carry

    lax.fori_loop(0, BLOCKS, patch_step, 0)

    rates = rate_rows(rate_ref, ROWS)
    place = lax.broadcasted_iota(jnp.int32, (MODES, ROWS), 1).astype(F32)
    for slot, offsets, operand in ((0, ROWS - 1.0 - place, gated), (1, place, d_conv)):
        high, low = split_bf16(jnp.exp(-rates * offsets))
        table = jnp.concatenate([high, low], axis=0).astype(BF16)
        product = jnp.dot(table, operand[...], preferred_element_type=F32)
        ends[slot * 8 : slot * 8 + 8, :] = product[:8] + product[8:]

    for part in range(NY):
        y_send[part] = ends[:, part * QUARTER : (part + 1) * QUARTER]

    def y_copy(source, target, step, slot):
        peer = lax.rem(y + step, NY)
        return pltpu.make_async_remote_copy(
            src_ref=source.at[peer],
            dst_ref=target.at[y],
            send_sem=send_sems.at[slot],
            recv_sem=recv_sems.at[slot],
            device_id={"ctx": z * NY + peer},
            device_id_type=MESH,
        )

    leaving = []

    def settle(target, number, slot):
        done = pltpu.make_async_remote_copy(
            src_ref=target.at[pl.ds(0, number)],
            dst_ref=target.at[pl.ds(0, number)],
            send_sem=send_sems.at[slot],
            recv_sem=recv_sems.at[slot],
            device_id={"ctx": z * NY + lax.rem(y + 1, NY)},
            device_id_type=MESH,
        )
        done.wait_recv()
        leaving.append(done)

    for step in range(1, NY):
        y_copy(y_send, y_recv, step, 0).start()
    y_recv[y] = y_send[y]

    place = lax.broadcasted_iota(jnp.int32, (MODES, ROWS), 1).astype(F32)
    weigh_fwd = jnp.exp(-rates * (place + 1.0)).astype(BF16)
    weigh_back = jnp.exp(-rates * (ROWS - place)).astype(BF16)

    def partner(branch, lanes):
        if branch == 0:
            return go_ref[:, lanes].astype(F32)
        return (short_v if branch == 1 else short_k)[0:ROWS, lanes]

    def moved_rows(branch, lanes):
        extended = jnp.concatenate(
            [before_tile(branch, lanes), inputs[branch][:, lanes].astype(F32)], axis=0
        )
        return [extended[8:]] + [pltpu.roll(extended, tap_at, 0)[8:] for tap_at in (1, 2)]

    def moment_step(block, carry):
        lanes = pl.ds(pl.multiple_of(block * WIDE, WIDE), WIDE)
        part = block // (QUARTER // WIDE)
        inner = pl.ds(pl.multiple_of(lax.rem(block, QUARTER // WIDE) * WIDE, WIDE), WIDE)
        for branch in range(3):
            weigh = weigh_back if branch else weigh_fwd
            other = partner(branch, lanes)
            for tap_at, moved in enumerate(moved_rows(branch, lanes)):
                product = jnp.dot(
                    weigh, (other * moved).astype(BF16), preferred_element_type=F32
                )
                m_send[part, branch * 3 + tap_at, :, inner] = product.astype(BF16)
        return carry

    lax.fori_loop(0, CHANNELS // WIDE, moment_step, 0)

    settle(y_recv, NY - 1, 0)

    speeds = rate_rows(rate_ref, QUARTER)
    step_decay = jnp.exp(-speeds * float(ROWS))
    group_decay = jnp.exp(-speeds * float(ROWS * NY))

    def fold(value):
        return jnp.concatenate([value[:, : QUARTER // 2], value[:, QUARTER // 2 :]], axis=0)

    def unfold(value):
        return jnp.concatenate([value[:8], value[8:]], axis=1)

    ahead_total = y_recv[0, 0:8]
    back_total = y_recv[NY - 1, 8:16]
    for index in range(1, NY):
        ahead_total = ahead_total * step_decay + y_recv[index, 0:8]
        back_total = back_total * step_decay + y_recv[NY - 1 - index, 8:16]
    z_send[0] = fold(ahead_total).astype(BF16)
    z_send[1] = fold(back_total).astype(BF16)

    def z_start(step, carry):
        peer = lax.rem(z + step, NZ)
        pltpu.make_async_remote_copy(
            src_ref=z_send.at[jnp.where(peer < z, 1, 0)],
            dst_ref=z_recv.at[z],
            send_sem=send_sems.at[1],
            recv_sem=recv_sems.at[1],
            device_id={"ctx": peer * NY + y},
            device_id_type=MESH,
        ).start()
        return carry

    lax.fori_loop(1, NZ, z_start, 0)
    z_recv[z] = jnp.zeros((16, QUARTER // 2), BF16)
    for step in range(1, NY):
        y_copy(m_send, m_recv, step, 8).start()
    m_recv[y] = m_send[y]

    row_at = lax.broadcasted_iota(jnp.int32, (ROWS, ROWS), 0)
    col_at = lax.broadcasted_iota(jnp.int32, (ROWS, ROWS), 1)
    for mode in range(MODES):
        speed = rate_ref[mode]
        here = slice(mode * ROWS, (mode + 1) * ROWS)
        for table, lag in ((fwd_table, row_at - col_at), (bwd_table, col_at - row_at)):
            power = jnp.exp(-speed * jnp.maximum(lag, 0).astype(F32))
            high, low = split_bf16(jnp.where(lag >= 0, power, 0.0))
            table[here, 0:ROWS] = high.astype(BF16)
            table[here, ROWS : 2 * ROWS] = low.astype(BF16)

    gain_rows = jnp.sqrt(1.0 - jnp.exp(-2.0 * rate_rows(rate_ref, WIDE)))

    def modal_step(block, carry):
        lanes = pl.ds(pl.multiple_of(block * WIDE, WIDE), WIDE)
        columns = residue_ref[:, lanes] * gain_rows
        source = gated[:, lanes]
        modal[...] = jnp.dot(
            fwd_table[...],
            jnp.concatenate([source, source], axis=0),
            preferred_element_type=F32,
        )
        cot = d_conv[:, lanes].astype(F32)
        total = jnp.zeros((ROWS, WIDE), F32)
        for mode in range(MODES):
            state = modal[mode * ROWS : (mode + 1) * ROWS, :]
            total = total + columns[mode : mode + 1] * state
            res_local[mode : mode + 1, lanes] = jnp.sum(cot * state, axis=0, keepdims=True)
        conv_local[:, lanes] = total
        source = d_conv[:, lanes]
        modal[...] = jnp.dot(
            bwd_table[...],
            jnp.concatenate([source, source], axis=0),
            preferred_element_type=F32,
        )
        total = jnp.zeros((ROWS, WIDE), F32)
        for mode in range(MODES):
            total = total + columns[mode : mode + 1] * modal[mode * ROWS : (mode + 1) * ROWS, :]
        back_local[:, lanes] = total
        return carry

    lax.fori_loop(0, CHANNELS // WIDE, modal_step, 0)

    def local_step(block, carry):
        lanes = pl.ds(pl.multiple_of(block * LANES, LANES), LANES)
        part = block // (QUARTER // LANES)
        inner = pl.ds(pl.multiple_of(lax.rem(block, QUARTER // LANES) * LANES, LANES), LANES)
        for branch in range(3):
            filtered = (back_local if branch else conv_local)[:, lanes]
            value = filtered * partner(branch, lanes)
            for tap_at, moved in enumerate(moved_rows(branch, lanes)):
                at = branch * 3 + tap_at
                l_send[part, at : at + 1, inner] = jnp.sum(value * moved, axis=0, keepdims=True)
        l_send[part, 9:17, inner] = res_local[:, lanes]
        return carry

    lax.fori_loop(0, BLOCKS, local_step, 0)
    for step in range(1, NY):
        y_copy(l_send, l_recv, step, 9).start()
    l_recv[y] = l_send[y]

    settle(z_recv, NZ - 1, 1)

    start = jnp.zeros((MODES, QUARTER), F32)
    finish = jnp.zeros((MODES, QUARTER), F32)
    for index in range(NZ):
        start = jnp.where(
            index < z, start * group_decay + unfold(z_recv[index].astype(F32)), start
        )
        other = NZ - 1 - index
        finish = jnp.where(
            other > z, finish * group_decay + unfold(z_recv[other].astype(F32)), finish
        )
    for index in range(NY):
        b_send[index, 0:8] = start
        start = start * step_decay + y_recv[index, 0:8]
        other = NY - 1 - index
        b_send[other, 8:16] = finish
        finish = finish * step_decay + y_recv[other, 8:16]

    for step in range(1, NY):
        y_copy(b_send, b_recv, step, 2).start()
    b_recv[y] = b_send[y]

    one = jnp.exp(-speeds)
    gains = jnp.sqrt(1.0 - jnp.exp(-2.0 * speeds))
    mine = pl.ds(pl.multiple_of(y * QUARTER, QUARTER), QUARTER)
    own_columns = residue_ref[:, mine] * gains
    settle(m_recv, NY - 1, 8)
    settle(l_recv, NY - 1, 9)
    local = l_recv[0]
    for index in range(1, NY):
        local = local + l_recv[index]
    pairs = jnp.zeros((MODES, QUARTER), F32)
    for index in range(NY):
        pairs = pairs + b_send[index, 0:8] * y_recv[index, 8:16]
    res_part = gains * (local[9:17] + one * pairs)
    for branch in range(3):
        half = slice(8, 16) if branch else slice(0, 8)
        for tap_at in range(3):
            at = branch * 3 + tap_at
            pairs = jnp.zeros((MODES, QUARTER), F32)
            for index in range(NY):
                pairs = pairs + b_send[index, half] * m_recv[index, at].astype(F32)
            row = local[at : at + 1] + jnp.sum(own_columns * pairs, axis=0, keepdims=True)
            for offset in range(NDP // 2):
                r_send[2 * offset, at : at + 1] = row[:, offset * LANES : (offset + 1) * LANES]
    for offset in range(NDP // 2):
        r_send[2 * offset + 1, 0:8] = res_part[:, offset * LANES : (offset + 1) * LANES]
        r_send[2 * offset + 1, 8:9] = jnp.zeros((1, LANES), F32)

    for step in range(1, NDP):
        peer = lax.rem(dp + step, NDP)
        pltpu.make_async_remote_copy(
            src_ref=r_send.at[peer],
            dst_ref=r_recv.at[dp],
            send_sem=send_sems.at[3],
            recv_sem=recv_sems.at[3],
            device_id={"dp": peer},
            device_id_type=MESH,
        ).start()
    r_recv[dp] = r_send[dp]
    settle(r_recv, NDP - 1, 3)
    total = r_recv[0]
    for index in range(1, NDP):
        total = total + r_recv[index]
    p_send[...] = total
    p_recv[z] = total

    core = lax.rem(dp, 2)
    block_here = y * (NDP // 2) + dp // 2
    res_home = jnp.logical_and(core == 1, block_here == z)

    def line_copy(peer):
        return pltpu.make_async_remote_copy(
            src_ref=p_send,
            dst_ref=p_recv.at[z],
            send_sem=send_sems.at[4],
            recv_sem=recv_sems.at[4],
            device_id={"ctx": peer * NY + y},
            device_id_type=MESH,
        )

    @pl.when(core == 0)
    def _():
        def line_start(step, carry):
            line_copy(lax.rem(z + step, NZ)).start()
            return carry

        lax.fori_loop(1, NZ, line_start, 0)

    @pl.when(jnp.logical_and(core == 1, block_here != z))
    def _():
        line_copy(block_here).start()

    settle(b_recv, NY - 1, 2)

    for part in range(NY):
        lanes = slice(part * QUARTER, (part + 1) * QUARTER)
        columns = residue_ref[:, lanes] * gains
        state = b_recv[part, 0:8]
        costate = b_recv[part, 8:16]
        for slot, value in ((0, columns * state), (1, columns * costate)):
            high, low = split_bf16(value)
            enter[slot, :, lanes] = jnp.concatenate([high, low, high, low], axis=0).astype(BF16)
        out_state = state * step_decay + ends[0:8, lanes]
        next_first = one * out_state + tail_gd[0:1, lanes]
        next_second = one * next_first + tail_gd[1:2, lanes]
        back_second = (costate - tail_gd[8:9, lanes]) / one
        edge[0:8, lanes] = two_row_tile(
            jnp.sum(columns * next_first, axis=0, keepdims=True),
            jnp.sum(columns * next_second, axis=0, keepdims=True),
            0,
        )
        edge[8:16, lanes] = two_row_tile(
            jnp.sum(columns * costate, axis=0, keepdims=True),
            jnp.sum(columns * back_second, axis=0, keepdims=True),
            0,
        )

    lane_at = lax.broadcasted_iota(jnp.int32, (ROWS, 4 * MODES), 1)
    lane_rate = jnp.zeros((ROWS, 4 * MODES), F32)
    for mode in range(MODES):
        lane_rate = jnp.where(lax.rem(lane_at, MODES) == mode, rate_ref[mode], lane_rate)
    place = lax.broadcasted_iota(jnp.int32, (ROWS, 4 * MODES), 0).astype(F32)

    def spread(offsets):
        high, low = split_bf16(jnp.exp(-lane_rate * offsets))
        return jnp.where(lane_at < 2 * MODES, high, low).astype(BF16)

    spread_fwd = spread(place + 1.0)
    spread_back = spread(ROWS - place)
    outs = (gq_ref, gk_ref, gv_ref)

    def final_step(block, carry):
        lanes = pl.ds(pl.multiple_of(block * LANES, LANES), LANES)
        conv = conv_local[:, lanes] + jnp.dot(
            spread_fwd, enter[0, :, lanes], preferred_element_type=F32
        )
        back = back_local[:, lanes] + jnp.dot(
            spread_back, enter[1, :, lanes], preferred_element_type=F32
        )
        conv_ext = jnp.concatenate([conv, edge[0:8, lanes]], axis=0)
        back_ext = jnp.concatenate([back, edge[8:16, lanes]], axis=0)
        cot = jnp.concatenate([go_ref[:, lanes].astype(F32), after_tile(3, lanes)], axis=0)
        mixed_ref[:, lanes] = (short_q[0:ROWS, lanes] * conv).astype(BF16)
        d_shorts = (cot * conv_ext, back_ext * short_v[:, lanes], back_ext * short_k[:, lanes])
        for branch in range(3):
            value = d_shorts[branch]
            first, second, third = taps(branch, lanes)
            total = (
                first * value[:ROWS]
                + second * pltpu.roll(value, ROWS + 8 - 1, 0)[:ROWS]
                + third * pltpu.roll(value, ROWS + 8 - 2, 0)[:ROWS]
            )
            outs[branch][:, lanes] = total.astype(BF16)
        return carry

    lax.fori_loop(0, BLOCKS, final_step, 0)
    stores = [
        pltpu.make_async_copy(source, target, store_sems.at[index])
        for index, (source, target) in enumerate(
            ((mixed_ref, mixed_hbm), (gq_ref, gq_hbm), (gk_ref, gk_hbm), (gv_ref, gv_hbm))
        )
    ]
    for store in stores:
        store.start()

    def await_line():
        done = pltpu.make_async_remote_copy(
            src_ref=p_recv.at[pl.ds(0, NZ - 1)],
            dst_ref=p_recv.at[pl.ds(0, NZ - 1)],
            send_sem=send_sems.at[4],
            recv_sem=recv_sems.at[4],
            device_id={"ctx": lax.rem(z + 1, NZ) * NY + y},
            device_id_type=MESH,
        )
        done.wait_recv()
        total = p_recv[0]
        for index in range(1, NZ):
            total = total + p_recv[index]
        return total

    def share_copy(source, target, slot, peer):
        peer_y, peer_dp = plane_peer(peer)
        return pltpu.make_async_remote_copy(
            src_ref=source,
            dst_ref=target,
            send_sem=send_sems.at[slot],
            recv_sem=recv_sems.at[slot],
            device_id={"ctx": z * NY + peer_y, "dp": peer_dp},
            device_id_type=MESH,
        )

    def share(source, target, slot):
        def start_one(step, carry):
            share_copy(source, target, slot, lax.rem(plane + step, PLANE)).start()
            return carry

        lax.fori_loop(1, PLANE, start_one, 0)

    @pl.when(core == 0)
    def _():
        short_sum[block_here] = await_line()
        share(short_sum.at[block_here], short_sum.at[block_here], 5)

    @pl.when(res_home)
    def _():
        res_sum[...] = await_line()
        share(res_sum, res_sum, 10)

    def await_short(number):
        here = short_sum.at[pl.ds(0, number)]
        next_peer = lax.rem(plane + 1, PLANE)
        share_copy(here, here, 5, next_peer).wait_recv()

    @pl.when(core == 0)
    def _():
        await_short(BLOCKS - 1)

    @pl.when(core == 1)
    def _():
        await_short(BLOCKS)

    @pl.when(jnp.logical_not(res_home))
    def _():
        share_copy(res_sum, res_sum, 10, lax.rem(plane + 1, PLANE)).wait_recv()

    for block in range(BLOCKS):
        lanes = slice(block * LANES, (block + 1) * LANES)
        for branch in range(3):
            gshort_ref[branch, :, lanes] = short_sum[block, 3 * branch : 3 * branch + 3]
    gres_ref[...] = pltpu.roll(res_sum[0:8], lax.rem(LANES - 32 * y, LANES), 1)[:, :32]
    for store in stores:
        store.wait()
    for copy in halos + leaving:
        copy.wait_send()

    @pl.when(core == 0)
    def _():
        def line_end(step, carry):
            line_copy(lax.rem(z + step, NZ)).wait_send()
            return carry

        def share_end(step, carry):
            here = short_sum.at[block_here]
            share_copy(here, here, 5, lax.rem(plane + step, PLANE)).wait_send()
            return carry

        lax.fori_loop(1, NZ, line_end, 0)
        lax.fori_loop(1, PLANE, share_end, 0)

    @pl.when(jnp.logical_and(core == 1, block_here != z))
    def _():
        line_copy(block_here).wait_send()

    @pl.when(res_home)
    def _():
        def share_end(step, carry):
            share_copy(res_sum, res_sum, 10, lax.rem(plane + step, PLANE)).wait_send()
            return carry

        lax.fori_loop(1, PLANE, share_end, 0)


def store_kernel(*refs):
    sources, targets, stages = refs[:6], refs[6:12], refs[12:18]
    load_sems, store_sems = refs[18:]
    loads = [
        pltpu.make_async_copy(source, stage, load_sems.at[index])
        for index, (source, stage) in enumerate(zip(sources, stages))
    ]
    stores = [
        pltpu.make_async_copy(stage, target, store_sems.at[index])
        for index, (stage, target) in enumerate(zip(stages, targets))
    ]
    for load in loads:
        load.start()
    for load, store in zip(loads, stores):
        load.wait()
        store.start()
    for store in stores:
        store.wait()


def shards(q_in, k_in, v_in, grad_out, short_filter, residue, rate):
    inputs = (q_in[0], k_in[0], v_in[0], grad_out[0])
    vmem = pl.BlockSpec(memory_space=pltpu.VMEM)
    smem = pl.BlockSpec(memory_space=pltpu.SMEM)
    hbm = pl.BlockSpec(memory_space=pltpu.HBM)
    block = jax.ShapeDtypeStruct((ROWS, CHANNELS), BF16)
    results = pl.pallas_call(
        operator_kernel,
        out_shape=(
            block,
            block,
            block,
            block,
            jax.ShapeDtypeStruct((MODES, 32), F32),
            jax.ShapeDtypeStruct((3, 3, CHANNELS), F32),
        ),
        in_specs=[smem] + [hbm] * 4 + [vmem] * 2,
        out_specs=(hbm,) * 4 + (vmem,) * 2,
        scratch_shapes=[pltpu.VMEM((ROWS, CHANNELS), BF16)] * 8
        + [pltpu.VMEM((8, CHANNELS), BF16)] * 4
        + [
            pltpu.VMEM((ROWS + 8, CHANNELS), F32),
            pltpu.VMEM((ROWS + 8, CHANNELS), F32),
            pltpu.VMEM((ROWS + 8, CHANNELS), F32),
            pltpu.VMEM((ROWS, CHANNELS), BF16),
            pltpu.VMEM((ROWS, CHANNELS), BF16),
            pltpu.VMEM((16, CHANNELS), F32),
            pltpu.VMEM((MODES * ROWS, 2 * ROWS), BF16),
            pltpu.VMEM((MODES * ROWS, 2 * ROWS), BF16),
            pltpu.VMEM((MODES * ROWS, WIDE), F32),
            pltpu.VMEM((ROWS, CHANNELS), F32),
            pltpu.VMEM((ROWS, CHANNELS), F32),
            pltpu.VMEM((MODES, CHANNELS), F32),
            pltpu.VMEM((16, CHANNELS), F32),
            pltpu.VMEM((NY, 16, QUARTER), F32),
            pltpu.VMEM((NY, 16, QUARTER), F32),
            pltpu.VMEM((2, 16, QUARTER // 2), BF16),
            pltpu.VMEM((NZ, 16, QUARTER // 2), BF16),
            pltpu.VMEM((NY, 16, QUARTER), F32),
            pltpu.VMEM((NY, 16, QUARTER), F32),
            pltpu.VMEM((2, 4 * MODES, CHANNELS), BF16),
            pltpu.VMEM((16, CHANNELS), F32),
            pltpu.VMEM((NY, 9, MODES, QUARTER), BF16),
            pltpu.VMEM((NY, 9, MODES, QUARTER), BF16),
            pltpu.VMEM((NY, 17, QUARTER), F32),
            pltpu.VMEM((NY, 17, QUARTER), F32),
            pltpu.VMEM((NDP, 9, LANES), F32),
            pltpu.VMEM((NDP, 9, LANES), F32),
            pltpu.VMEM((9, LANES), F32),
            pltpu.VMEM((NZ, 9, LANES), F32),
            pltpu.VMEM((BLOCKS, 9, LANES), F32),
            pltpu.VMEM((9, LANES), F32),
            pltpu.SemaphoreType.DMA((4,)),
            pltpu.SemaphoreType.DMA((4,)),
            pltpu.SemaphoreType.DMA((11,)),
            pltpu.SemaphoreType.DMA((11,)),
        ],
        name="operator",
        compiler_params=pltpu.CompilerParams(
            collective_id=0, has_side_effects=True, vmem_limit_bytes=GRANT
        ),
    )(rate, *inputs, short_filter, residue.T)
    mixed, gq, gk, gv, gres, gshort = pl.pallas_call(
        store_kernel,
        out_shape=tuple(jax.ShapeDtypeStruct(item.shape, item.dtype) for item in results),
        in_specs=[hbm] * 6,
        out_specs=(hbm,) * 6,
        scratch_shapes=[pltpu.VMEM(item.shape, item.dtype) for item in results]
        + [pltpu.SemaphoreType.DMA((6,))] * 2,
        name="store",
        compiler_params=pltpu.CompilerParams(vmem_limit_bytes=GRANT),
    )(*results)
    return (
        mixed[None],
        gq[None],
        gk[None],
        gv[None],
        gres.T,
        gshort,
    )


def solution(mesh):
    placed = P("dp", "ctx", None)
    return jax.shard_map(
        shards,
        mesh=mesh,
        in_specs=(placed, placed, placed, placed, P(), P(), P()),
        out_specs=(placed, placed, placed, placed, P("ctx", None), P()),
        check_vma=False,
    )
```

```python
import functools

import jax
import jax.numpy as jnp
from jax import lax
from jax.experimental import pallas as pl
from jax.experimental.pallas import tpu as pltpu
from jax.sharding import PartitionSpec as P

MESH = pl.DeviceIdType.MESH
ROWS = 128
CHANNELS = 2048
MODES = 8
LANES = 128
BLOCKS = CHANNELS // LANES
WIDE = 256
NZ = 16
NY = 4
NDP = 8
PLANE = NY * NDP
QUARTER = CHANNELS // NY
GRANT = 56 << 20
F32 = jnp.float32
BF16 = jnp.bfloat16


def split_bf16(value):
    high = value.astype(BF16).astype(F32)
    return high, value - high


def two_row_tile(first, second, at):
    width = first.shape[1]
    row = lax.broadcasted_iota(jnp.int32, (8, width), 0)
    return jnp.where(row == at, first, jnp.where(row == at + 1, second, 0.0))


def rate_rows(rate_ref, width):
    row = lax.broadcasted_iota(jnp.int32, (MODES, width), 0)
    total = jnp.zeros((MODES, width), F32)
    for mode in range(MODES):
        total = jnp.where(row == mode, rate_ref[mode], total)
    return total


def farthest_first(index):
    half = (index + 1) // 2
    return NZ // 2 + half * (1 - 2 * lax.rem(index, 2))


PLANE_STEPS = [
    (dy, dx, core)
    for dy, dx, core in sorted(
        ((dy, dx, core) for dy in range(NY) for dx in range(NDP // 2) for core in range(2)),
        key=lambda at: (-min(at[0], NY - at[0]) - min(at[1], NDP // 2 - at[1]), at),
    )
    if (dy, dx, core) != (0, 0, 0)
]


def operator_kernel(
    rate_ref,
    q_hbm,
    k_hbm,
    v_hbm,
    go_hbm,
    filter_ref,
    residue_ref,
    mixed_hbm,
    gq_hbm,
    gk_hbm,
    gv_hbm,
    gres_ref,
    gshort_ref,
    mixed_ref,
    gq_ref,
    gk_ref,
    gv_ref,
    q_ref,
    k_ref,
    v_ref,
    go_ref,
    tail_send,
    head_send,
    tail_recv,
    head_recv,
    short_q,
    short_k,
    short_v,
    gated,
    d_conv,
    tail_gd,
    fwd_table,
    bwd_table,
    modal,
    conv_local,
    back_local,
    res_local,
    ends,
    y_send,
    y_recv,
    z_send,
    z_recv,
    b_send,
    b_recv,
    enter,
    edge,
    m_send,
    m_recv,
    l_send,
    l_recv,
    r_send,
    r_recv,
    p_send,
    p_recv,
    short_sum,
    res_sum,
    load_sems,
    store_sems,
    send_sems,
    recv_sems,
):
    ctx = lax.axis_index("ctx")
    dp = lax.axis_index("dp")
    z = ctx // NY
    y = lax.rem(ctx, NY)

    inputs = (q_ref, k_ref, v_ref, go_ref)
    loads = [
        pltpu.make_async_copy(source, target, load_sems.at[index])
        for index, (source, target) in enumerate(zip((q_hbm, k_hbm, v_hbm, go_hbm), inputs))
    ]
    for load in loads:
        load.start()

    barrier = pltpu.get_barrier_semaphore()
    count = NZ * NY
    following = lax.rem(ctx + 1, count)
    preceding = lax.rem(ctx + count - 1, count)
    column = dp // 2
    core = lax.rem(dp, 2)

    def line_peer(index):
        return lax.rem(z + farthest_first(index), NZ)

    def plane_device(step):
        dy, dx, dcore = step
        peer_x = lax.rem(column + dx, NDP // 2)
        peer_core = (1 - core) if dcore else core
        return {"ctx": z * NY + lax.rem(y + dy, NY), "dp": peer_x * 2 + peer_core}

    def greet_line(index, carry):
        pl.semaphore_signal(
            barrier, inc=1, device_id={"ctx": line_peer(index) * NY + y}, device_id_type=MESH
        )
        return carry

    lax.fori_loop(0, NZ - 1, greet_line, 0)
    for step in PLANE_STEPS:
        pl.semaphore_signal(
            barrier, inc=1, device_id=plane_device(step), device_id_type=MESH
        )
    for neighbour in (following, preceding):
        pl.semaphore_signal(
            barrier, inc=1, device_id={"ctx": neighbour}, device_id_type=MESH
        )

    def taps(branch, lanes):
        return [filter_ref[branch, j : j + 1, lanes] for j in range(3)]

    row_at = lax.broadcasted_iota(jnp.int32, (ROWS, ROWS), 0)
    col_at = lax.broadcasted_iota(jnp.int32, (ROWS, ROWS), 1)
    for mode in range(MODES):
        speed = rate_ref[mode]
        here = slice(mode * ROWS, (mode + 1) * ROWS)
        for table, lag in ((fwd_table, row_at - col_at), (bwd_table, col_at - row_at)):
            power = jnp.exp(-speed * jnp.maximum(lag, 0).astype(F32))
            high, low = split_bf16(jnp.where(lag >= 0, power, 0.0))
            table[here, 0:ROWS] = high.astype(BF16)
            table[here, ROWS : 2 * ROWS] = low.astype(BF16)

    for load in loads:
        load.wait()

    row_eight = lax.broadcasted_iota(jnp.int32, (8, CHANNELS), 0)
    tails = jnp.zeros((8, CHANNELS), F32)
    heads = jnp.zeros((8, CHANNELS), F32)
    for branch in range(4):
        last = inputs[branch][ROWS - 16 : ROWS, :].astype(F32)
        first = inputs[branch][0:16, :].astype(F32)
        for index in range(2):
            here = row_eight == 2 * branch + index
            heads = jnp.where(here, first[index : index + 1], heads)
            if branch < 3:
                tails = jnp.where(here, last[14 + index : 15 + index], tails)
    tail_send[...] = tails.astype(BF16)
    head_send[...] = heads.astype(BF16)

    pl.semaphore_wait(barrier, NZ - 1 + PLANE - 1 + 2)
    halos = [
        pltpu.make_async_remote_copy(
            src_ref=source,
            dst_ref=target,
            send_sem=send_sems.at[slot],
            recv_sem=recv_sems.at[slot],
            device_id={"ctx": neighbour},
            device_id_type=MESH,
        )
        for slot, source, target, neighbour in (
            (6, tail_send, tail_recv, following),
            (7, head_send, head_recv, preceding),
        )
    ]
    for halo in halos:
        halo.start()

    def before_tile(branch, lanes):
        rows = tail_recv[:, lanes].astype(F32)[2 * branch : 2 * branch + 2]
        tile = two_row_tile(rows[0:1], rows[1:2], 6)
        return jnp.where(ctx == 0, 0.0, tile)

    def after_tile(branch, lanes):
        rows = head_recv[:, lanes].astype(F32)[2 * branch : 2 * branch + 2]
        tile = two_row_tile(rows[0:1], rows[1:2], 0)
        return jnp.where(ctx == count - 1, 0.0, tile)

    shorts = (short_q, short_k, short_v)

    def convolve(branch, lanes, extended):
        first, second, third = taps(branch, lanes)
        return (
            first * extended[8:]
            + second * pltpu.roll(extended, 1, 0)[8:]
            + third * pltpu.roll(extended, 2, 0)[8:]
        )

    def short_step(block, carry):
        lanes = pl.ds(pl.multiple_of(block * LANES, LANES), LANES)
        results = []
        for branch in range(3):
            values = inputs[branch][:, lanes].astype(F32)
            extended = jnp.concatenate([jnp.zeros((8, LANES), F32), values], axis=0)
            total = convolve(branch, lanes, extended)
            shorts[branch][0:ROWS, lanes] = total
            results.append(total)
        query, keyed, valued = results
        gated[:, lanes] = (keyed * valued).astype(BF16)
        d_conv[:, lanes] = (go_ref[:, lanes].astype(F32) * query).astype(BF16)
        return carry

    lax.fori_loop(0, BLOCKS, short_step, 0)

    for halo in halos:
        halo.wait_recv()

    def patch_step(block, carry):
        lanes = pl.ds(pl.multiple_of(block * LANES, LANES), LANES)
        firsts = []
        nexts = []
        for branch in range(3):
            values = inputs[branch][0:16, lanes].astype(F32)
            extended = jnp.concatenate([before_tile(branch, lanes), values], axis=0)
            firsts.append(convolve(branch, lanes, extended))
            shorts[branch][0:16, lanes] = firsts[branch]
            values = inputs[branch][ROWS - 16 : ROWS, lanes].astype(F32)[8:]
            extended = jnp.concatenate([values, after_tile(branch, lanes)], axis=0)
            nexts.append(convolve(branch, lanes, extended))
            shorts[branch][ROWS : ROWS + 8, lanes] = nexts[branch]
        gated[0:16, lanes] = (firsts[1] * firsts[2]).astype(BF16)
        d_conv[0:16, lanes] = (go_ref[0:16, lanes].astype(F32) * firsts[0]).astype(BF16)
        tail_gd[0:8, lanes] = (nexts[1] * nexts[2]).astype(BF16).astype(F32)
        tail_gd[8:16, lanes] = (after_tile(3, lanes) * nexts[0]).astype(BF16).astype(F32)
        return carry

    lax.fori_loop(0, BLOCKS, patch_step, 0)

    rates = rate_rows(rate_ref, ROWS)
    place = lax.broadcasted_iota(jnp.int32, (MODES, ROWS), 1).astype(F32)
    for slot, offsets, operand in ((0, ROWS - 1.0 - place, gated), (1, place, d_conv)):
        high, low = split_bf16(jnp.exp(-rates * offsets))
        table = jnp.concatenate([high, low], axis=0).astype(BF16)
        product = jnp.dot(table, operand[...], preferred_element_type=F32)
        ends[slot * 8 : slot * 8 + 8, :] = product[:8] + product[8:]

    for part in range(NY):
        y_send[part] = ends[:, part * QUARTER : (part + 1) * QUARTER]

    def y_copy(source, target, step, slot):
        peer = lax.rem(y + step, NY)
        return pltpu.make_async_remote_copy(
            src_ref=source.at[peer],
            dst_ref=target.at[y],
            send_sem=send_sems.at[slot],
            recv_sem=recv_sems.at[slot],
            device_id={"ctx": z * NY + peer},
            device_id_type=MESH,
        )

    leaving = []

    def settle(target, number, slot):
        done = pltpu.make_async_remote_copy(
            src_ref=target.at[pl.ds(0, number)],
            dst_ref=target.at[pl.ds(0, number)],
            send_sem=send_sems.at[slot],
            recv_sem=recv_sems.at[slot],
            device_id={"ctx": z * NY + lax.rem(y + 1, NY)},
            device_id_type=MESH,
        )
        done.wait_recv()
        leaving.append(done)

    for step in range(1, NY):
        y_copy(y_send, y_recv, step, 0).start()
    y_recv[y] = y_send[y]

    place = lax.broadcasted_iota(jnp.int32, (MODES, ROWS), 1).astype(F32)
    weigh_fwd = jnp.exp(-rates * (place + 1.0)).astype(BF16)
    weigh_back = jnp.exp(-rates * (ROWS - place)).astype(BF16)

    def partner(branch, lanes):
        if branch == 0:
            return go_ref[:, lanes].astype(F32)
        return (short_v if branch == 1 else short_k)[0:ROWS, lanes]

    def moved_rows(branch, lanes):
        extended = jnp.concatenate(
            [before_tile(branch, lanes), inputs[branch][:, lanes].astype(F32)], axis=0
        )
        return [extended[8:]] + [pltpu.roll(extended, tap_at, 0)[8:] for tap_at in (1, 2)]

    def moment_step(block, carry):
        lanes = pl.ds(pl.multiple_of(block * WIDE, WIDE), WIDE)
        part = block // (QUARTER // WIDE)
        inner = pl.ds(pl.multiple_of(lax.rem(block, QUARTER // WIDE) * WIDE, WIDE), WIDE)
        for branch in range(3):
            weigh = weigh_back if branch else weigh_fwd
            other = partner(branch, lanes)
            for tap_at, moved in enumerate(moved_rows(branch, lanes)):
                product = jnp.dot(
                    weigh, (other * moved).astype(BF16), preferred_element_type=F32
                )
                m_send[part, branch * 3 + tap_at, :, inner] = product.astype(BF16)
        return carry

    lax.fori_loop(0, CHANNELS // WIDE, moment_step, 0)

    settle(y_recv, NY - 1, 0)

    speeds = rate_rows(rate_ref, QUARTER)
    step_decay = jnp.exp(-speeds * float(ROWS))
    group_decay = jnp.exp(-speeds * float(ROWS * NY))

    def fold(value):
        return jnp.concatenate([value[:, : QUARTER // 2], value[:, QUARTER // 2 :]], axis=0)

    def unfold(value):
        return jnp.concatenate([value[:8], value[8:]], axis=1)

    ahead_total = y_recv[0, 0:8]
    back_total = y_recv[NY - 1, 8:16]
    for index in range(1, NY):
        ahead_total = ahead_total * step_decay + y_recv[index, 0:8]
        back_total = back_total * step_decay + y_recv[NY - 1 - index, 8:16]
    z_send[0] = fold(ahead_total).astype(BF16)
    z_send[1] = fold(back_total).astype(BF16)

    def z_start(index, carry):
        peer = line_peer(index)
        pltpu.make_async_remote_copy(
            src_ref=z_send.at[jnp.where(peer < z, 1, 0)],
            dst_ref=z_recv.at[z],
            send_sem=send_sems.at[1],
            recv_sem=recv_sems.at[1],
            device_id={"ctx": peer * NY + y},
            device_id_type=MESH,
        ).start()
        return carry

    lax.fori_loop(0, NZ - 1, z_start, 0)
    z_recv[z] = jnp.zeros((16, QUARTER // 2), BF16)
    for step in range(1, NY):
        y_copy(m_send, m_recv, step, 8).start()
    m_recv[y] = m_send[y]

    gain_rows = jnp.sqrt(1.0 - jnp.exp(-2.0 * rate_rows(rate_ref, WIDE)))

    def modal_step(block, carry):
        lanes = pl.ds(pl.multiple_of(block * WIDE, WIDE), WIDE)
        columns = residue_ref[:, lanes] * gain_rows
        source = gated[:, lanes]
        modal[...] = jnp.dot(
            fwd_table[...],
            jnp.concatenate([source, source], axis=0),
            preferred_element_type=F32,
        )
        cot = d_conv[:, lanes].astype(F32)
        total = jnp.zeros((ROWS, WIDE), F32)
        for mode in range(MODES):
            state = modal[mode * ROWS : (mode + 1) * ROWS, :]
            total = total + columns[mode : mode + 1] * state
            res_local[mode : mode + 1, lanes] = jnp.sum(cot * state, axis=0, keepdims=True)
        conv_local[:, lanes] = total
        source = d_conv[:, lanes]
        modal[...] = jnp.dot(
            bwd_table[...],
            jnp.concatenate([source, source], axis=0),
            preferred_element_type=F32,
        )
        total = jnp.zeros((ROWS, WIDE), F32)
        for mode in range(MODES):
            total = total + columns[mode : mode + 1] * modal[mode * ROWS : (mode + 1) * ROWS, :]
        back_local[:, lanes] = total
        return carry

    lax.fori_loop(0, CHANNELS // WIDE, modal_step, 0)

    def local_step(block, carry):
        lanes = pl.ds(pl.multiple_of(block * LANES, LANES), LANES)
        for branch in range(3):
            filtered = (back_local if branch else conv_local)[:, lanes]
            value = filtered * partner(branch, lanes)
            for tap_at, moved in enumerate(moved_rows(branch, lanes)):
                at = branch * 3 + tap_at
                l_send[2 * block, at : at + 1] = jnp.sum(value * moved, axis=0, keepdims=True)
        l_send[2 * block + 1, 0:8] = res_local[:, lanes] * gain_rows[:, :LANES]
        l_send[2 * block + 1, 8:9] = jnp.zeros((1, LANES), F32)
        return carry

    lax.fori_loop(0, BLOCKS, local_step, 0)

    plane = y * NDP + dp
    for step in PLANE_STEPS:
        where = plane_device(step)
        piece = lax.rem(y + step[0], NY) * NDP + where["dp"]
        pltpu.make_async_remote_copy(
            src_ref=l_send.at[piece],
            dst_ref=l_recv.at[plane],
            send_sem=send_sems.at[9],
            recv_sem=recv_sems.at[9],
            device_id=where,
            device_id_type=MESH,
        ).start()
    l_recv[plane] = l_send[plane]

    settle(z_recv, NZ - 1, 1)

    start = jnp.zeros((MODES, QUARTER), F32)
    finish = jnp.zeros((MODES, QUARTER), F32)
    for index in range(NZ):
        start = jnp.where(
            index < z, start * group_decay + unfold(z_recv[index].astype(F32)), start
        )
        other = NZ - 1 - index
        finish = jnp.where(
            other > z, finish * group_decay + unfold(z_recv[other].astype(F32)), finish
        )
    for index in range(NY):
        b_send[index, 0:8] = start
        start = start * step_decay + y_recv[index, 0:8]
        other = NY - 1 - index
        b_send[other, 8:16] = finish
        finish = finish * step_decay + y_recv[other, 8:16]

    for step in range(1, NY):
        y_copy(b_send, b_recv, step, 2).start()
    b_recv[y] = b_send[y]

    one = jnp.exp(-speeds)
    gains = jnp.sqrt(1.0 - jnp.exp(-2.0 * speeds))
    mine = pl.ds(pl.multiple_of(y * QUARTER, QUARTER), QUARTER)
    own_columns = residue_ref[:, mine] * gains
    settle(m_recv, NY - 1, 8)
    pairs = jnp.zeros((MODES, QUARTER), F32)
    for index in range(NY):
        pairs = pairs + b_send[index, 0:8] * y_recv[index, 8:16]
    res_part = gains * one * pairs
    for branch in range(3):
        half = slice(8, 16) if branch else slice(0, 8)
        for tap_at in range(3):
            at = branch * 3 + tap_at
            pairs = jnp.zeros((MODES, QUARTER), F32)
            for index in range(NY):
                pairs = pairs + b_send[index, half] * m_recv[index, at].astype(F32)
            row = jnp.sum(own_columns * pairs, axis=0, keepdims=True)
            for offset in range(NDP // 2):
                r_send[2 * offset, at : at + 1] = row[:, offset * LANES : (offset + 1) * LANES]
    for offset in range(NDP // 2):
        r_send[2 * offset + 1, 0:8] = res_part[:, offset * LANES : (offset + 1) * LANES]
        r_send[2 * offset + 1, 8:9] = jnp.zeros((1, LANES), F32)

    for step in range(1, NDP):
        peer = lax.rem(dp + step, NDP)
        pltpu.make_async_remote_copy(
            src_ref=r_send.at[peer],
            dst_ref=r_recv.at[dp],
            send_sem=send_sems.at[3],
            recv_sem=recv_sems.at[3],
            device_id={"dp": peer},
            device_id_type=MESH,
        ).start()
    r_recv[dp] = r_send[dp]
    settle(r_recv, NDP - 1, 3)
    settle(l_recv, PLANE - 1, 9)
    total = r_recv[0]
    for index in range(1, NDP):
        total = total + r_recv[index]
    for index in range(PLANE):
        total = total + l_recv[index]
    p_send[...] = total
    p_recv[z] = total

    block_here = y * (NDP // 2) + column
    res_home = jnp.logical_and(core == 1, block_here == z)

    def line_copy(peer):
        return pltpu.make_async_remote_copy(
            src_ref=p_send,
            dst_ref=p_recv.at[z],
            send_sem=send_sems.at[4],
            recv_sem=recv_sems.at[4],
            device_id={"ctx": peer * NY + y},
            device_id_type=MESH,
        )

    @pl.when(core == 0)
    def _():
        def line_start(index, carry):
            line_copy(line_peer(index)).start()
            return carry

        lax.fori_loop(0, NZ - 1, line_start, 0)

    @pl.when(jnp.logical_and(core == 1, block_here != z))
    def _():
        line_copy(block_here).start()

    settle(b_recv, NY - 1, 2)

    for part in range(NY):
        lanes = slice(part * QUARTER, (part + 1) * QUARTER)
        columns = residue_ref[:, lanes] * gains
        state = b_recv[part, 0:8]
        costate = b_recv[part, 8:16]
        for slot, value in ((0, columns * state), (1, columns * costate)):
            high, low = split_bf16(value)
            enter[slot, :, lanes] = jnp.concatenate([high, low, high, low], axis=0).astype(BF16)
        out_state = state * step_decay + ends[0:8, lanes]
        next_first = one * out_state + tail_gd[0:1, lanes]
        next_second = one * next_first + tail_gd[1:2, lanes]
        back_second = (costate - tail_gd[8:9, lanes]) / one
        edge[0:8, lanes] = two_row_tile(
            jnp.sum(columns * next_first, axis=0, keepdims=True),
            jnp.sum(columns * next_second, axis=0, keepdims=True),
            0,
        )
        edge[8:16, lanes] = two_row_tile(
            jnp.sum(columns * costate, axis=0, keepdims=True),
            jnp.sum(columns * back_second, axis=0, keepdims=True),
            0,
        )

    lane_at = lax.broadcasted_iota(jnp.int32, (ROWS, 4 * MODES), 1)
    lane_rate = jnp.zeros((ROWS, 4 * MODES), F32)
    for mode in range(MODES):
        lane_rate = jnp.where(lax.rem(lane_at, MODES) == mode, rate_ref[mode], lane_rate)
    place = lax.broadcasted_iota(jnp.int32, (ROWS, 4 * MODES), 0).astype(F32)

    def spread(offsets):
        high, low = split_bf16(jnp.exp(-lane_rate * offsets))
        return jnp.where(lane_at < 2 * MODES, high, low).astype(BF16)

    spread_fwd = spread(place + 1.0)
    spread_back = spread(ROWS - place)
    outs = (gq_ref, gk_ref, gv_ref)

    def final_step(block, carry):
        lanes = pl.ds(pl.multiple_of(block * LANES, LANES), LANES)
        conv = conv_local[:, lanes] + jnp.dot(
            spread_fwd, enter[0, :, lanes], preferred_element_type=F32
        )
        back = back_local[:, lanes] + jnp.dot(
            spread_back, enter[1, :, lanes], preferred_element_type=F32
        )
        conv_ext = jnp.concatenate([conv, edge[0:8, lanes]], axis=0)
        back_ext = jnp.concatenate([back, edge[8:16, lanes]], axis=0)
        cot = jnp.concatenate([go_ref[:, lanes].astype(F32), after_tile(3, lanes)], axis=0)
        mixed_ref[:, lanes] = (short_q[0:ROWS, lanes] * conv).astype(BF16)
        d_shorts = (cot * conv_ext, back_ext * short_v[:, lanes], back_ext * short_k[:, lanes])
        for branch in range(3):
            value = d_shorts[branch]
            first, second, third = taps(branch, lanes)
            total = (
                first * value[:ROWS]
                + second * pltpu.roll(value, ROWS + 8 - 1, 0)[:ROWS]
                + third * pltpu.roll(value, ROWS + 8 - 2, 0)[:ROWS]
            )
            outs[branch][:, lanes] = total.astype(BF16)
        return carry

    lax.fori_loop(0, BLOCKS, final_step, 0)
    stores = [
        pltpu.make_async_copy(source, target, store_sems.at[index])
        for index, (source, target) in enumerate(
            ((mixed_ref, mixed_hbm), (gq_ref, gq_hbm), (gk_ref, gk_hbm), (gv_ref, gv_hbm))
        )
    ]
    for store in stores:
        store.start()

    def await_line():
        done = pltpu.make_async_remote_copy(
            src_ref=p_recv.at[pl.ds(0, NZ - 1)],
            dst_ref=p_recv.at[pl.ds(0, NZ - 1)],
            send_sem=send_sems.at[4],
            recv_sem=recv_sems.at[4],
            device_id={"ctx": lax.rem(z + 1, NZ) * NY + y},
            device_id_type=MESH,
        )
        done.wait_recv()
        total = p_recv[0]
        for index in range(1, NZ):
            total = total + p_recv[index]
        return total

    def share_copy(source, target, slot, step):
        return pltpu.make_async_remote_copy(
            src_ref=source,
            dst_ref=target,
            send_sem=send_sems.at[slot],
            recv_sem=recv_sems.at[slot],
            device_id=plane_device(step),
            device_id_type=MESH,
        )

    def share(source, target, slot):
        for step in PLANE_STEPS:
            share_copy(source, target, slot, step).start()

    @pl.when(core == 0)
    def _():
        short_sum[block_here] = await_line()
        share(short_sum.at[block_here], short_sum.at[block_here], 5)

    @pl.when(res_home)
    def _():
        res_sum[...] = await_line()
        share(res_sum, res_sum, 10)

    def await_short(number):
        here = short_sum.at[pl.ds(0, number)]
        share_copy(here, here, 5, PLANE_STEPS[0]).wait_recv()

    @pl.when(core == 0)
    def _():
        await_short(BLOCKS - 1)

    @pl.when(core == 1)
    def _():
        await_short(BLOCKS)

    @pl.when(jnp.logical_not(res_home))
    def _():
        share_copy(res_sum, res_sum, 10, PLANE_STEPS[0]).wait_recv()

    for block in range(BLOCKS):
        lanes = slice(block * LANES, (block + 1) * LANES)
        for branch in range(3):
            gshort_ref[branch, :, lanes] = short_sum[block, 3 * branch : 3 * branch + 3]
    gres_ref[...] = pltpu.roll(res_sum[0:8], lax.rem(LANES - 32 * y, LANES), 1)[:, :32]
    for store in stores:
        store.wait()
    for copy in halos + leaving:
        copy.wait_send()

    @pl.when(core == 0)
    def _():
        here = p_recv.at[pl.ds(0, NZ - 1)]
        pltpu.make_async_remote_copy(
            src_ref=here,
            dst_ref=here,
            send_sem=send_sems.at[4],
            recv_sem=recv_sems.at[4],
            device_id={"ctx": line_peer(0) * NY + y},
            device_id_type=MESH,
        ).wait_send()
        for step in PLANE_STEPS:
            share_copy(short_sum.at[block_here], short_sum.at[block_here], 5, step).wait_send()

    @pl.when(jnp.logical_and(core == 1, block_here != z))
    def _():
        line_copy(block_here).wait_send()

    @pl.when(res_home)
    def _():
        for step in PLANE_STEPS:
            share_copy(res_sum, res_sum, 10, step).wait_send()


def store_kernel(*refs):
    sources, targets, stages = refs[:6], refs[6:12], refs[12:18]
    load_sems, store_sems = refs[18:]
    pieces = []
    for source, target, stage in zip(sources, targets, stages):
        rows = source.shape[0]
        for first in range(0, source.shape[0], rows):
            here = pl.ds(first, rows)
            pieces.append((source.at[here], stage.at[here], target.at[here], len(pieces)))
    loads = [
        pltpu.make_async_copy(source, stage, load_sems.at[at]) for source, stage, _, at in pieces
    ]
    stores = [
        pltpu.make_async_copy(stage, target, store_sems.at[at]) for _, stage, target, at in pieces
    ]
    for load in loads:
        load.start()
    for load, store in zip(loads, stores):
        load.wait()
        store.start()
    for store in stores:
        store.wait()


def shards(q_in, k_in, v_in, grad_out, short_filter, residue, rate):
    inputs = (q_in[0], k_in[0], v_in[0], grad_out[0])
    vmem = pl.BlockSpec(memory_space=pltpu.VMEM)
    smem = pl.BlockSpec(memory_space=pltpu.SMEM)
    hbm = pl.BlockSpec(memory_space=pltpu.HBM)
    block = jax.ShapeDtypeStruct((ROWS, CHANNELS), BF16)
    results = pl.pallas_call(
        operator_kernel,
        out_shape=(
            block,
            block,
            block,
            block,
            jax.ShapeDtypeStruct((MODES, 32), F32),
            jax.ShapeDtypeStruct((3, 3, CHANNELS), F32),
        ),
        in_specs=[smem] + [hbm] * 4 + [vmem] * 2,
        out_specs=(hbm,) * 4 + (vmem,) * 2,
        scratch_shapes=[pltpu.VMEM((ROWS, CHANNELS), BF16)] * 8
        + [pltpu.VMEM((8, CHANNELS), BF16)] * 4
        + [
            pltpu.VMEM((ROWS + 8, CHANNELS), F32),
            pltpu.VMEM((ROWS + 8, CHANNELS), F32),
            pltpu.VMEM((ROWS + 8, CHANNELS), F32),
            pltpu.VMEM((ROWS, CHANNELS), BF16),
            pltpu.VMEM((ROWS, CHANNELS), BF16),
            pltpu.VMEM((16, CHANNELS), F32),
            pltpu.VMEM((MODES * ROWS, 2 * ROWS), BF16),
            pltpu.VMEM((MODES * ROWS, 2 * ROWS), BF16),
            pltpu.VMEM((MODES * ROWS, WIDE), F32),
            pltpu.VMEM((ROWS, CHANNELS), F32),
            pltpu.VMEM((ROWS, CHANNELS), F32),
            pltpu.VMEM((MODES, CHANNELS), F32),
            pltpu.VMEM((16, CHANNELS), F32),
            pltpu.VMEM((NY, 16, QUARTER), F32),
            pltpu.VMEM((NY, 16, QUARTER), F32),
            pltpu.VMEM((2, 16, QUARTER // 2), BF16),
            pltpu.VMEM((NZ, 16, QUARTER // 2), BF16),
            pltpu.VMEM((NY, 16, QUARTER), F32),
            pltpu.VMEM((NY, 16, QUARTER), F32),
            pltpu.VMEM((2, 4 * MODES, CHANNELS), BF16),
            pltpu.VMEM((16, CHANNELS), F32),
            pltpu.VMEM((NY, 9, MODES, QUARTER), BF16),
            pltpu.VMEM((NY, 9, MODES, QUARTER), BF16),
            pltpu.VMEM((PLANE, 9, LANES), F32),
            pltpu.VMEM((PLANE, 9, LANES), F32),
            pltpu.VMEM((NDP, 9, LANES), F32),
            pltpu.VMEM((NDP, 9, LANES), F32),
            pltpu.VMEM((9, LANES), F32),
            pltpu.VMEM((NZ, 9, LANES), F32),
            pltpu.VMEM((BLOCKS, 9, LANES), F32),
            pltpu.VMEM((9, LANES), F32),
            pltpu.SemaphoreType.DMA((4,)),
            pltpu.SemaphoreType.DMA((4,)),
            pltpu.SemaphoreType.DMA((11,)),
            pltpu.SemaphoreType.DMA((11,)),
        ],
        name="operator",
        compiler_params=pltpu.CompilerParams(
            collective_id=0, has_side_effects=True, vmem_limit_bytes=GRANT
        ),
    )(rate, *inputs, short_filter, residue.T)
    mixed, gq, gk, gv, gres, gshort = pl.pallas_call(
        store_kernel,
        out_shape=tuple(jax.ShapeDtypeStruct(item.shape, item.dtype) for item in results),
        in_specs=[hbm] * 6,
        out_specs=(hbm,) * 6,
        scratch_shapes=[pltpu.VMEM(item.shape, item.dtype) for item in results]
        + [pltpu.SemaphoreType.DMA((6,))] * 2,
        name="store",
        compiler_params=pltpu.CompilerParams(vmem_limit_bytes=GRANT),
    )(*results)
    return (
        mixed[None],
        gq[None],
        gk[None],
        gv[None],
        gres.T,
        gshort,
    )


def solution(mesh):
    placed = P("dp", "ctx", None)
    return jax.shard_map(
        shards,
        mesh=mesh,
        in_specs=(placed, placed, placed, placed, P(), P(), P()),
        out_specs=(placed, placed, placed, placed, P("ctx", None), P()),
        check_vma=False,
    )
```

```python
import functools

import jax
import jax.numpy as jnp
from jax import lax
from jax.experimental import pallas as pl
from jax.experimental.pallas import tpu as pltpu
from jax.sharding import PartitionSpec as P

MESH = pl.DeviceIdType.MESH
ROWS = 128
CHANNELS = 2048
MODES = 8
LANES = 128
BLOCKS = CHANNELS // LANES
WIDE = 256
NZ = 16
NY = 4
NDP = 8
PLANE = NY * NDP
QUARTER = CHANNELS // NY
GRANT = 56 << 20
F32 = jnp.float32
BF16 = jnp.bfloat16


def split_bf16(value):
    high = value.astype(BF16).astype(F32)
    return high, value - high


def two_row_tile(first, second, at):
    width = first.shape[1]
    row = lax.broadcasted_iota(jnp.int32, (8, width), 0)
    return jnp.where(row == at, first, jnp.where(row == at + 1, second, 0.0))


def rate_rows(rate_ref, width):
    row = lax.broadcasted_iota(jnp.int32, (MODES, width), 0)
    total = jnp.zeros((MODES, width), F32)
    for mode in range(MODES):
        total = jnp.where(row == mode, rate_ref[mode], total)
    return total


def farthest_first(index):
    half = (index + 1) // 2
    return NZ // 2 + half * (1 - 2 * lax.rem(index, 2))


PLANE_STEPS = [
    (dy, dx, core)
    for dy, dx, core in sorted(
        ((dy, dx, core) for dy in range(NY) for dx in range(NDP // 2) for core in range(2)),
        key=lambda at: (-min(at[0], NY - at[0]) - min(at[1], NDP // 2 - at[1]), at),
    )
    if (dy, dx, core) != (0, 0, 0)
]


def operator_kernel(
    rate_ref,
    q_hbm,
    k_hbm,
    v_hbm,
    go_hbm,
    filter_ref,
    residue_ref,
    mixed_hbm,
    gq_hbm,
    gk_hbm,
    gv_hbm,
    gres_ref,
    gshort_ref,
    mixed_ref,
    gq_ref,
    gk_ref,
    gv_ref,
    q_ref,
    k_ref,
    v_ref,
    go_ref,
    tail_send,
    head_send,
    tail_recv,
    head_recv,
    short_q,
    short_k,
    short_v,
    gated,
    d_conv,
    tail_gd,
    fwd_table,
    bwd_table,
    modal,
    conv_local,
    back_local,
    res_local,
    ends,
    y_send,
    y_recv,
    z_send,
    z_recv,
    b_send,
    b_recv,
    enter,
    edge,
    e_send,
    e_recv,
    e_prev,
    m_send,
    m_recv,
    l_send,
    l_recv,
    r_send,
    r_recv,
    p_send,
    p_recv,
    short_sum,
    res_sum,
    load_sems,
    store_sems,
    send_sems,
    recv_sems,
):
    ctx = lax.axis_index("ctx")
    dp = lax.axis_index("dp")
    z = ctx // NY
    y = lax.rem(ctx, NY)

    inputs = (q_ref, k_ref, v_ref, go_ref)
    loads = [
        pltpu.make_async_copy(source, target, load_sems.at[index])
        for index, (source, target) in enumerate(zip((q_hbm, k_hbm, v_hbm, go_hbm), inputs))
    ]
    for load in loads:
        load.start()

    barrier = pltpu.get_barrier_semaphore()
    count = NZ * NY
    following = lax.rem(ctx + 1, count)
    preceding = lax.rem(ctx + count - 1, count)
    column = dp // 2
    core = lax.rem(dp, 2)

    def line_peer(index):
        return lax.rem(z + farthest_first(index), NZ)

    def plane_device(step):
        dy, dx, dcore = step
        peer_x = lax.rem(column + dx, NDP // 2)
        peer_core = (1 - core) if dcore else core
        return {"ctx": z * NY + lax.rem(y + dy, NY), "dp": peer_x * 2 + peer_core}

    def greet_line(index, carry):
        pl.semaphore_signal(
            barrier, inc=1, device_id={"ctx": line_peer(index) * NY + y}, device_id_type=MESH
        )
        return carry

    lax.fori_loop(0, NZ - 1, greet_line, 0)
    for step in PLANE_STEPS:
        pl.semaphore_signal(
            barrier, inc=1, device_id=plane_device(step), device_id_type=MESH
        )
    for neighbour in (following, preceding):
        pl.semaphore_signal(
            barrier, inc=1, device_id={"ctx": neighbour}, device_id_type=MESH
        )

    @pl.when(jnp.logical_or(y == 1, y == 2))
    def _():
        sender = lax.rem(z + NZ - 1, NZ) * NY + NY - 1
        pl.semaphore_signal(barrier, inc=1, device_id={"ctx": sender}, device_id_type=MESH)

    def taps(branch, lanes):
        return [filter_ref[branch, j : j + 1, lanes] for j in range(3)]

    row_at = lax.broadcasted_iota(jnp.int32, (ROWS, ROWS), 0)
    col_at = lax.broadcasted_iota(jnp.int32, (ROWS, ROWS), 1)
    for mode in range(MODES):
        speed = rate_ref[mode]
        here = slice(mode * ROWS, (mode + 1) * ROWS)
        for table, lag in ((fwd_table, row_at - col_at), (bwd_table, col_at - row_at)):
            power = jnp.exp(-speed * jnp.maximum(lag, 0).astype(F32))
            high, low = split_bf16(jnp.where(lag >= 0, power, 0.0))
            table[here, 0:ROWS] = high.astype(BF16)
            table[here, ROWS : 2 * ROWS] = low.astype(BF16)

    for load in loads:
        load.wait()

    row_eight = lax.broadcasted_iota(jnp.int32, (8, CHANNELS), 0)
    tails = jnp.zeros((8, CHANNELS), F32)
    heads = jnp.zeros((8, CHANNELS), F32)
    for branch in range(4):
        last = inputs[branch][ROWS - 16 : ROWS, :].astype(F32)
        first = inputs[branch][0:16, :].astype(F32)
        for index in range(2):
            here = row_eight == 2 * branch + index
            heads = jnp.where(here, first[index : index + 1], heads)
            if branch < 3:
                tails = jnp.where(here, last[14 + index : 15 + index], tails)
    tail_send[...] = tails.astype(BF16)
    head_send[...] = heads.astype(BF16)
    edges = jnp.concatenate([tails, heads], axis=0).astype(BF16)
    for part in range(NY):
        e_send[part] = edges[:, part * QUARTER : (part + 1) * QUARTER]

    def before_tile(branch, lanes):
        rows = tail_recv[:, lanes].astype(F32)[2 * branch : 2 * branch + 2]
        tile = two_row_tile(rows[0:1], rows[1:2], 6)
        return jnp.where(ctx == 0, 0.0, tile)

    def after_tile(branch, lanes):
        rows = head_recv[:, lanes].astype(F32)[2 * branch : 2 * branch + 2]
        tile = two_row_tile(rows[0:1], rows[1:2], 0)
        return jnp.where(ctx == count - 1, 0.0, tile)

    shorts = (short_q, short_k, short_v)

    def convolve(branch, lanes, extended):
        first, second, third = taps(branch, lanes)
        return (
            first * extended[8:]
            + second * pltpu.roll(extended, 1, 0)[8:]
            + third * pltpu.roll(extended, 2, 0)[8:]
        )

    def short_step(block, carry):
        lanes = pl.ds(pl.multiple_of(block * LANES, LANES), LANES)
        results = []
        for branch in range(3):
            values = inputs[branch][:, lanes].astype(F32)
            extended = jnp.concatenate([jnp.zeros((8, LANES), F32), values], axis=0)
            total = convolve(branch, lanes, extended)
            shorts[branch][0:ROWS, lanes] = total
            results.append(total)
        query, keyed, valued = results
        gated[:, lanes] = (keyed * valued).astype(BF16)
        d_conv[:, lanes] = (go_ref[:, lanes].astype(F32) * query).astype(BF16)
        return carry

    lax.fori_loop(0, BLOCKS, short_step, 0)

    rates = rate_rows(rate_ref, ROWS)
    place = lax.broadcasted_iota(jnp.int32, (MODES, ROWS), 1).astype(F32)
    def compute_ends():
        for slot, offsets, operand in ((0, ROWS - 1.0 - place, gated), (1, place, d_conv)):
            high, low = split_bf16(jnp.exp(-rates * offsets))
            table = jnp.concatenate([high, low], axis=0).astype(BF16)
            product = jnp.dot(table, operand[...], preferred_element_type=F32)
            ends[slot * 8 : slot * 8 + 8, :] = product[:8] + product[8:]

    compute_ends()

    for part in range(NY):
        y_send[part] = ends[:, part * QUARTER : (part + 1) * QUARTER]

    pl.semaphore_wait(barrier, NZ - 1 + PLANE - 1 + 2 + 2 * (y // (NY - 1)))

    def y_copy(source, target, step, slot):
        peer = lax.rem(y + step, NY)
        return pltpu.make_async_remote_copy(
            src_ref=source.at[peer],
            dst_ref=target.at[y],
            send_sem=send_sems.at[slot],
            recv_sem=recv_sems.at[slot],
            device_id={"ctx": z * NY + peer},
            device_id_type=MESH,
        )

    leaving = []

    def settle(target, number, slot):
        done = pltpu.make_async_remote_copy(
            src_ref=target.at[pl.ds(0, number)],
            dst_ref=target.at[pl.ds(0, number)],
            send_sem=send_sems.at[slot],
            recv_sem=recv_sems.at[slot],
            device_id={"ctx": z * NY + lax.rem(y + 1, NY)},
            device_id_type=MESH,
        )
        done.wait_recv()
        leaving.append(done)

    for step in range(1, NY):
        y_copy(y_send, y_recv, step, 0).start()
    y_recv[y] = y_send[y]
    for step in range(1, NY):
        y_copy(e_send, e_recv, step, 11).start()
    e_recv[y] = e_send[y]

    def onward_copy(part):
        return pltpu.make_async_remote_copy(
            src_ref=e_send.at[part],
            dst_ref=e_prev,
            send_sem=send_sems.at[12],
            recv_sem=recv_sems.at[12],
            device_id={"ctx": lax.rem(z + 1, NZ) * NY + part},
            device_id_type=MESH,
        )

    @pl.when(y == NY - 1)
    def _():
        for part in range(NY):
            onward_copy(part).start()

    halos = [
        pltpu.make_async_remote_copy(
            src_ref=source,
            dst_ref=target,
            send_sem=send_sems.at[slot],
            recv_sem=recv_sems.at[slot],
            device_id={"ctx": neighbour},
            device_id_type=MESH,
        )
        for slot, source, target, neighbour in (
            (6, tail_send, tail_recv, following),
            (7, head_send, head_recv, preceding),
        )
    ]
    for halo in halos:
        halo.start()

    gain_rows = jnp.sqrt(1.0 - jnp.exp(-2.0 * rate_rows(rate_ref, WIDE)))

    def back_step(block, carry):
        lanes = pl.ds(pl.multiple_of(block * WIDE, WIDE), WIDE)
        columns = residue_ref[:, lanes] * gain_rows
        source = d_conv[:, lanes]
        modal[...] = jnp.dot(
            bwd_table[...],
            jnp.concatenate([source, source], axis=0),
            preferred_element_type=F32,
        )
        total = jnp.zeros((ROWS, WIDE), F32)
        for mode in range(MODES):
            total = total + columns[mode : mode + 1] * modal[mode * ROWS : (mode + 1) * ROWS, :]
        back_local[:, lanes] = total
        return carry

    lax.fori_loop(0, CHANNELS // WIDE, back_step, 0)

    settle(y_recv, NY - 1, 0)

    speeds = rate_rows(rate_ref, QUARTER)
    settle(e_recv, NY - 1, 11)
    onward_copy(0).wait_recv()

    mine = pl.ds(pl.multiple_of(y * QUARTER, QUARTER), QUARTER)
    own_taps = [taps(branch, mine) for branch in range(3)]

    def rounded(value):
        return value.astype(BF16).astype(F32)

    for index in range(NY):
        here = e_recv[index].astype(F32)[8:16]
        prior = (e_recv[index - 1] if index else e_prev[...]).astype(F32)[0:8]
        if index == 0:
            prior = jnp.where(z == 0, 0.0, prior)
        plain = []
        full = []
        for branch in range(3):
            first, second, third = own_taps[branch]
            row0, row1 = (here[2 * branch + at : 2 * branch + at + 1] for at in range(2))
            old0, old1 = (prior[2 * branch + at : 2 * branch + at + 1] for at in range(2))
            plain.append((first * row0, first * row1 + second * row0))
            full.append(
                (
                    first * row0 + second * old1 + third * old0,
                    first * row1 + second * row0 + third * old1,
                )
            )
        d_gate = []
        d_out = []
        for at in range(2):
            cot = here[6 + at : 7 + at]
            d_gate.append(
                rounded(full[1][at] * full[2][at]) - rounded(plain[1][at] * plain[2][at])
            )
            d_out.append(rounded(cot * full[0][at]) - rounded(cot * plain[0][at]))
        y_recv[index, 0:8] = (
            y_recv[index, 0:8]
            + jnp.exp(-speeds * (ROWS - 1.0)) * d_gate[0]
            + jnp.exp(-speeds * (ROWS - 2.0)) * d_gate[1]
        )
        y_recv[index, 8:16] = y_recv[index, 8:16] + d_out[0] + jnp.exp(-speeds) * d_out[1]

    step_decay = jnp.exp(-speeds * float(ROWS))
    group_decay = jnp.exp(-speeds * float(ROWS * NY))

    def fold(value):
        return jnp.concatenate([value[:, : QUARTER // 2], value[:, QUARTER // 2 :]], axis=0)

    def unfold(value):
        return jnp.concatenate([value[:8], value[8:]], axis=1)

    ahead_total = y_recv[0, 0:8]
    back_total = y_recv[NY - 1, 8:16]
    for index in range(1, NY):
        ahead_total = ahead_total * step_decay + y_recv[index, 0:8]
        back_total = back_total * step_decay + y_recv[NY - 1 - index, 8:16]
    z_send[0] = fold(ahead_total).astype(BF16)
    z_send[1] = fold(back_total).astype(BF16)

    def z_start(index, carry):
        peer = line_peer(index)
        pltpu.make_async_remote_copy(
            src_ref=z_send.at[jnp.where(peer < z, 1, 0)],
            dst_ref=z_recv.at[z],
            send_sem=send_sems.at[1],
            recv_sem=recv_sems.at[1],
            device_id={"ctx": peer * NY + y},
            device_id_type=MESH,
        ).start()
        return carry

    lax.fori_loop(0, NZ - 1, z_start, 0)
    z_recv[z] = jnp.zeros((16, QUARTER // 2), BF16)
    for halo in halos:
        halo.wait_recv()

    def patch_step(block, carry):
        lanes = pl.ds(pl.multiple_of(block * LANES, LANES), LANES)
        firsts = []
        nexts = []
        for branch in range(3):
            values = inputs[branch][0:16, lanes].astype(F32)
            extended = jnp.concatenate([before_tile(branch, lanes), values], axis=0)
            firsts.append(convolve(branch, lanes, extended))
            shorts[branch][0:16, lanes] = firsts[branch]
            values = inputs[branch][ROWS - 16 : ROWS, lanes].astype(F32)[8:]
            extended = jnp.concatenate([values, after_tile(branch, lanes)], axis=0)
            nexts.append(convolve(branch, lanes, extended))
            shorts[branch][ROWS : ROWS + 8, lanes] = nexts[branch]
        gated[0:16, lanes] = (firsts[1] * firsts[2]).astype(BF16)
        fresh = (go_ref[0:16, lanes].astype(F32) * firsts[0]).astype(BF16)
        change = fresh.astype(F32) - d_conv[0:16, lanes].astype(F32)
        d_conv[0:16, lanes] = fresh
        columns = residue_ref[:, lanes] * gain_rows[:, :LANES]
        whole = jnp.sum(columns, axis=0, keepdims=True)
        decayed = jnp.sum(columns * jnp.exp(-rates), axis=0, keepdims=True)
        back_local[0:8, lanes] = back_local[0:8, lanes] + two_row_tile(
            whole * change[0:1] + decayed * change[1:2], whole * change[1:2], 0
        )
        tail_gd[0:8, lanes] = (nexts[1] * nexts[2]).astype(BF16).astype(F32)
        tail_gd[8:16, lanes] = (after_tile(3, lanes) * nexts[0]).astype(BF16).astype(F32)
        return carry

    lax.fori_loop(0, BLOCKS, patch_step, 0)

    compute_ends()

    place = lax.broadcasted_iota(jnp.int32, (MODES, ROWS), 1).astype(F32)
    weigh_fwd = jnp.exp(-rates * (place + 1.0)).astype(BF16)
    weigh_back = jnp.exp(-rates * (ROWS - place)).astype(BF16)

    def partner(branch, lanes):
        if branch == 0:
            return go_ref[:, lanes].astype(F32)
        return (short_v if branch == 1 else short_k)[0:ROWS, lanes]

    def moved_rows(branch, lanes):
        extended = jnp.concatenate(
            [before_tile(branch, lanes), inputs[branch][:, lanes].astype(F32)], axis=0
        )
        return [extended[8:]] + [pltpu.roll(extended, tap_at, 0)[8:] for tap_at in (1, 2)]

    def moment_step(block, carry):
        lanes = pl.ds(pl.multiple_of(block * WIDE, WIDE), WIDE)
        part = block // (QUARTER // WIDE)
        inner = pl.ds(pl.multiple_of(lax.rem(block, QUARTER // WIDE) * WIDE, WIDE), WIDE)
        for branch in range(3):
            weigh = weigh_back if branch else weigh_fwd
            other = partner(branch, lanes)
            for tap_at, moved in enumerate(moved_rows(branch, lanes)):
                product = jnp.dot(
                    weigh, (other * moved).astype(BF16), preferred_element_type=F32
                )
                m_send[part, branch * 3 + tap_at, :, inner] = product.astype(BF16)
        return carry

    lax.fori_loop(0, CHANNELS // WIDE, moment_step, 0)

    for step in range(1, NY):
        y_copy(m_send, m_recv, step, 8).start()
    m_recv[y] = m_send[y]

    def modal_step(block, carry):
        lanes = pl.ds(pl.multiple_of(block * WIDE, WIDE), WIDE)
        columns = residue_ref[:, lanes] * gain_rows
        source = gated[:, lanes]
        modal[...] = jnp.dot(
            fwd_table[...],
            jnp.concatenate([source, source], axis=0),
            preferred_element_type=F32,
        )
        cot = d_conv[:, lanes].astype(F32)
        total = jnp.zeros((ROWS, WIDE), F32)
        for mode in range(MODES):
            state = modal[mode * ROWS : (mode + 1) * ROWS, :]
            total = total + columns[mode : mode + 1] * state
            res_local[mode : mode + 1, lanes] = jnp.sum(cot * state, axis=0, keepdims=True)
        conv_local[:, lanes] = total
        return carry

    lax.fori_loop(0, CHANNELS // WIDE, modal_step, 0)

    def local_step(block, carry):
        lanes = pl.ds(pl.multiple_of(block * LANES, LANES), LANES)
        for branch in range(3):
            filtered = (back_local if branch else conv_local)[:, lanes]
            value = filtered * partner(branch, lanes)
            for tap_at, moved in enumerate(moved_rows(branch, lanes)):
                at = branch * 3 + tap_at
                l_send[2 * block, at : at + 1] = jnp.sum(value * moved, axis=0, keepdims=True)
        l_send[2 * block + 1, 0:8] = res_local[:, lanes] * gain_rows[:, :LANES]
        l_send[2 * block + 1, 8:9] = jnp.zeros((1, LANES), F32)
        return carry

    lax.fori_loop(0, BLOCKS, local_step, 0)

    plane = y * NDP + dp
    for step in PLANE_STEPS:
        where = plane_device(step)
        piece = lax.rem(y + step[0], NY) * NDP + where["dp"]
        pltpu.make_async_remote_copy(
            src_ref=l_send.at[piece],
            dst_ref=l_recv.at[plane],
            send_sem=send_sems.at[9],
            recv_sem=recv_sems.at[9],
            device_id=where,
            device_id_type=MESH,
        ).start()
    l_recv[plane] = l_send[plane]

    settle(z_recv, NZ - 1, 1)

    start = jnp.zeros((MODES, QUARTER), F32)
    finish = jnp.zeros((MODES, QUARTER), F32)
    for index in range(NZ):
        start = jnp.where(
            index < z, start * group_decay + unfold(z_recv[index].astype(F32)), start
        )
        other = NZ - 1 - index
        finish = jnp.where(
            other > z, finish * group_decay + unfold(z_recv[other].astype(F32)), finish
        )
    for index in range(NY):
        b_send[index, 0:8] = start
        start = start * step_decay + y_recv[index, 0:8]
        other = NY - 1 - index
        b_send[other, 8:16] = finish
        finish = finish * step_decay + y_recv[other, 8:16]

    for step in range(1, NY):
        y_copy(b_send, b_recv, step, 2).start()
    b_recv[y] = b_send[y]

    one = jnp.exp(-speeds)
    gains = jnp.sqrt(1.0 - jnp.exp(-2.0 * speeds))
    own_columns = residue_ref[:, mine] * gains
    settle(m_recv, NY - 1, 8)
    pairs = jnp.zeros((MODES, QUARTER), F32)
    for index in range(NY):
        pairs = pairs + b_send[index, 0:8] * y_recv[index, 8:16]
    res_part = gains * one * pairs
    for branch in range(3):
        half = slice(8, 16) if branch else slice(0, 8)
        for tap_at in range(3):
            at = branch * 3 + tap_at
            pairs = jnp.zeros((MODES, QUARTER), F32)
            for index in range(NY):
                pairs = pairs + b_send[index, half] * m_recv[index, at].astype(F32)
            row = jnp.sum(own_columns * pairs, axis=0, keepdims=True)
            for offset in range(NDP // 2):
                r_send[2 * offset, at : at + 1] = row[:, offset * LANES : (offset + 1) * LANES]
    for offset in range(NDP // 2):
        r_send[2 * offset + 1, 0:8] = res_part[:, offset * LANES : (offset + 1) * LANES]
        r_send[2 * offset + 1, 8:9] = jnp.zeros((1, LANES), F32)

    for step in range(1, NDP):
        peer = lax.rem(dp + step, NDP)
        pltpu.make_async_remote_copy(
            src_ref=r_send.at[peer],
            dst_ref=r_recv.at[dp],
            send_sem=send_sems.at[3],
            recv_sem=recv_sems.at[3],
            device_id={"dp": peer},
            device_id_type=MESH,
        ).start()
    r_recv[dp] = r_send[dp]
    settle(r_recv, NDP - 1, 3)
    settle(l_recv, PLANE - 1, 9)
    total = r_recv[0]
    for index in range(1, NDP):
        total = total + r_recv[index]
    for index in range(PLANE):
        total = total + l_recv[index]
    p_send[...] = total
    p_recv[z] = total

    block_here = y * (NDP // 2) + column
    res_home = jnp.logical_and(core == 1, block_here == z)

    def line_copy(peer):
        return pltpu.make_async_remote_copy(
            src_ref=p_send,
            dst_ref=p_recv.at[z],
            send_sem=send_sems.at[4],
            recv_sem=recv_sems.at[4],
            device_id={"ctx": peer * NY + y},
            device_id_type=MESH,
        )

    @pl.when(core == 0)
    def _():
        def line_start(index, carry):
            line_copy(line_peer(index)).start()
            return carry

        lax.fori_loop(0, NZ - 1, line_start, 0)

    @pl.when(jnp.logical_and(core == 1, block_here != z))
    def _():
        line_copy(block_here).start()

    settle(b_recv, NY - 1, 2)

    for part in range(NY):
        lanes = slice(part * QUARTER, (part + 1) * QUARTER)
        columns = residue_ref[:, lanes] * gains
        state = b_recv[part, 0:8]
        costate = b_recv[part, 8:16]
        for slot, value in ((0, columns * state), (1, columns * costate)):
            high, low = split_bf16(value)
            enter[slot, :, lanes] = jnp.concatenate([high, low, high, low], axis=0).astype(BF16)
        out_state = state * step_decay + ends[0:8, lanes]
        next_first = one * out_state + tail_gd[0:1, lanes]
        next_second = one * next_first + tail_gd[1:2, lanes]
        back_second = (costate - tail_gd[8:9, lanes]) / one
        edge[0:8, lanes] = two_row_tile(
            jnp.sum(columns * next_first, axis=0, keepdims=True),
            jnp.sum(columns * next_second, axis=0, keepdims=True),
            0,
        )
        edge[8:16, lanes] = two_row_tile(
            jnp.sum(columns * costate, axis=0, keepdims=True),
            jnp.sum(columns * back_second, axis=0, keepdims=True),
            0,
        )

    lane_at = lax.broadcasted_iota(jnp.int32, (ROWS, 4 * MODES), 1)
    lane_rate = jnp.zeros((ROWS, 4 * MODES), F32)
    for mode in range(MODES):
        lane_rate = jnp.where(lax.rem(lane_at, MODES) == mode, rate_ref[mode], lane_rate)
    place = lax.broadcasted_iota(jnp.int32, (ROWS, 4 * MODES), 0).astype(F32)

    def spread(offsets):
        high, low = split_bf16(jnp.exp(-lane_rate * offsets))
        return jnp.where(lane_at < 2 * MODES, high, low).astype(BF16)

    spread_fwd = spread(place + 1.0)
    spread_back = spread(ROWS - place)
    outs = (gq_ref, gk_ref, gv_ref)

    def final_step(block, carry):
        lanes = pl.ds(pl.multiple_of(block * LANES, LANES), LANES)
        conv = conv_local[:, lanes] + jnp.dot(
            spread_fwd, enter[0, :, lanes], preferred_element_type=F32
        )
        back = back_local[:, lanes] + jnp.dot(
            spread_back, enter[1, :, lanes], preferred_element_type=F32
        )
        conv_ext = jnp.concatenate([conv, edge[0:8, lanes]], axis=0)
        back_ext = jnp.concatenate([back, edge[8:16, lanes]], axis=0)
        cot = jnp.concatenate([go_ref[:, lanes].astype(F32), after_tile(3, lanes)], axis=0)
        mixed_ref[:, lanes] = (short_q[0:ROWS, lanes] * conv).astype(BF16)
        d_shorts = (cot * conv_ext, back_ext * short_v[:, lanes], back_ext * short_k[:, lanes])
        for branch in range(3):
            value = d_shorts[branch]
            first, second, third = taps(branch, lanes)
            total = (
                first * value[:ROWS]
                + second * pltpu.roll(value, ROWS + 8 - 1, 0)[:ROWS]
                + third * pltpu.roll(value, ROWS + 8 - 2, 0)[:ROWS]
            )
            outs[branch][:, lanes] = total.astype(BF16)
        return carry

    lax.fori_loop(0, BLOCKS, final_step, 0)
    stores = [
        pltpu.make_async_copy(source, target, store_sems.at[index])
        for index, (source, target) in enumerate(
            ((mixed_ref, mixed_hbm), (gq_ref, gq_hbm), (gk_ref, gk_hbm), (gv_ref, gv_hbm))
        )
    ]
    for store in stores:
        store.start()

    def await_line():
        done = pltpu.make_async_remote_copy(
            src_ref=p_recv.at[pl.ds(0, NZ - 1)],
            dst_ref=p_recv.at[pl.ds(0, NZ - 1)],
            send_sem=send_sems.at[4],
            recv_sem=recv_sems.at[4],
            device_id={"ctx": lax.rem(z + 1, NZ) * NY + y},
            device_id_type=MESH,
        )
        done.wait_recv()
        total = p_recv[0]
        for index in range(1, NZ):
            total = total + p_recv[index]
        return total

    def share_copy(source, target, slot, step):
        return pltpu.make_async_remote_copy(
            src_ref=source,
            dst_ref=target,
            send_sem=send_sems.at[slot],
            recv_sem=recv_sems.at[slot],
            device_id=plane_device(step),
            device_id_type=MESH,
        )

    def share(source, target, slot):
        for step in PLANE_STEPS:
            share_copy(source, target, slot, step).start()

    @pl.when(core == 0)
    def _():
        short_sum[block_here] = await_line()
        share(short_sum.at[block_here], short_sum.at[block_here], 5)

    @pl.when(res_home)
    def _():
        res_sum[...] = await_line()
        share(res_sum, res_sum, 10)

    def await_short(number):
        here = short_sum.at[pl.ds(0, number)]
        share_copy(here, here, 5, PLANE_STEPS[0]).wait_recv()

    @pl.when(core == 0)
    def _():
        await_short(BLOCKS - 1)

    @pl.when(core == 1)
    def _():
        await_short(BLOCKS)

    @pl.when(jnp.logical_not(res_home))
    def _():
        share_copy(res_sum, res_sum, 10, PLANE_STEPS[0]).wait_recv()

    for block in range(BLOCKS):
        lanes = slice(block * LANES, (block + 1) * LANES)
        for branch in range(3):
            gshort_ref[branch, :, lanes] = short_sum[block, 3 * branch : 3 * branch + 3]
    gres_ref[...] = pltpu.roll(res_sum[0:8], lax.rem(LANES - 32 * y, LANES), 1)[:, :32]
    for store in stores:
        store.wait()
    for copy in halos + leaving:
        copy.wait_send()

    @pl.when(y == NY - 1)
    def _():
        for part in range(NY):
            onward_copy(part).wait_send()

    @pl.when(core == 0)
    def _():
        here = p_recv.at[pl.ds(0, NZ - 1)]
        pltpu.make_async_remote_copy(
            src_ref=here,
            dst_ref=here,
            send_sem=send_sems.at[4],
            recv_sem=recv_sems.at[4],
            device_id={"ctx": line_peer(0) * NY + y},
            device_id_type=MESH,
        ).wait_send()
        for step in PLANE_STEPS:
            share_copy(short_sum.at[block_here], short_sum.at[block_here], 5, step).wait_send()

    @pl.when(jnp.logical_and(core == 1, block_here != z))
    def _():
        line_copy(block_here).wait_send()

    @pl.when(res_home)
    def _():
        for step in PLANE_STEPS:
            share_copy(res_sum, res_sum, 10, step).wait_send()


def store_kernel(*refs):
    sources, targets, stages = refs[:6], refs[6:12], refs[12:18]
    load_sems, store_sems = refs[18:]
    pieces = []
    for source, target, stage in zip(sources, targets, stages):
        rows = source.shape[0]
        for first in range(0, source.shape[0], rows):
            here = pl.ds(first, rows)
            pieces.append((source.at[here], stage.at[here], target.at[here], len(pieces)))
    loads = [
        pltpu.make_async_copy(source, stage, load_sems.at[at]) for source, stage, _, at in pieces
    ]
    stores = [
        pltpu.make_async_copy(stage, target, store_sems.at[at]) for _, stage, target, at in pieces
    ]
    for load in loads:
        load.start()
    for load, store in zip(loads, stores):
        load.wait()
        store.start()
    for store in stores:
        store.wait()


def shards(q_in, k_in, v_in, grad_out, short_filter, residue, rate):
    inputs = (q_in[0], k_in[0], v_in[0], grad_out[0])
    vmem = pl.BlockSpec(memory_space=pltpu.VMEM)
    smem = pl.BlockSpec(memory_space=pltpu.SMEM)
    hbm = pl.BlockSpec(memory_space=pltpu.HBM)
    block = jax.ShapeDtypeStruct((ROWS, CHANNELS), BF16)
    results = pl.pallas_call(
        operator_kernel,
        out_shape=(
            block,
            block,
            block,
            block,
            jax.ShapeDtypeStruct((MODES, 32), F32),
            jax.ShapeDtypeStruct((3, 3, CHANNELS), F32),
        ),
        in_specs=[smem] + [hbm] * 4 + [vmem] * 2,
        out_specs=(hbm,) * 4 + (vmem,) * 2,
        scratch_shapes=[pltpu.VMEM((ROWS, CHANNELS), BF16)] * 8
        + [pltpu.VMEM((8, CHANNELS), BF16)] * 4
        + [
            pltpu.VMEM((ROWS + 8, CHANNELS), F32),
            pltpu.VMEM((ROWS + 8, CHANNELS), F32),
            pltpu.VMEM((ROWS + 8, CHANNELS), F32),
            pltpu.VMEM((ROWS, CHANNELS), BF16),
            pltpu.VMEM((ROWS, CHANNELS), BF16),
            pltpu.VMEM((16, CHANNELS), F32),
            pltpu.VMEM((MODES * ROWS, 2 * ROWS), BF16),
            pltpu.VMEM((MODES * ROWS, 2 * ROWS), BF16),
            pltpu.VMEM((MODES * ROWS, WIDE), F32),
            pltpu.VMEM((ROWS, CHANNELS), F32),
            pltpu.VMEM((ROWS, CHANNELS), F32),
            pltpu.VMEM((MODES, CHANNELS), F32),
            pltpu.VMEM((16, CHANNELS), F32),
            pltpu.VMEM((NY, 16, QUARTER), F32),
            pltpu.VMEM((NY, 16, QUARTER), F32),
            pltpu.VMEM((2, 16, QUARTER // 2), BF16),
            pltpu.VMEM((NZ, 16, QUARTER // 2), BF16),
            pltpu.VMEM((NY, 16, QUARTER), F32),
            pltpu.VMEM((NY, 16, QUARTER), F32),
            pltpu.VMEM((2, 4 * MODES, CHANNELS), BF16),
            pltpu.VMEM((16, CHANNELS), F32),
            pltpu.VMEM((NY, 16, QUARTER), BF16),
            pltpu.VMEM((NY, 16, QUARTER), BF16),
            pltpu.VMEM((16, QUARTER), BF16),
            pltpu.VMEM((NY, 9, MODES, QUARTER), BF16),
            pltpu.VMEM((NY, 9, MODES, QUARTER), BF16),
            pltpu.VMEM((PLANE, 9, LANES), F32),
            pltpu.VMEM((PLANE, 9, LANES), F32),
            pltpu.VMEM((NDP, 9, LANES), F32),
            pltpu.VMEM((NDP, 9, LANES), F32),
            pltpu.VMEM((9, LANES), F32),
            pltpu.VMEM((NZ, 9, LANES), F32),
            pltpu.VMEM((BLOCKS, 9, LANES), F32),
            pltpu.VMEM((9, LANES), F32),
            pltpu.SemaphoreType.DMA((4,)),
            pltpu.SemaphoreType.DMA((4,)),
            pltpu.SemaphoreType.DMA((13,)),
            pltpu.SemaphoreType.DMA((13,)),
        ],
        name="operator",
        compiler_params=pltpu.CompilerParams(
            collective_id=0, has_side_effects=True, vmem_limit_bytes=GRANT
        ),
    )(rate, *inputs, short_filter, residue.T)
    mixed, gq, gk, gv, gres, gshort = pl.pallas_call(
        store_kernel,
        out_shape=tuple(jax.ShapeDtypeStruct(item.shape, item.dtype) for item in results),
        in_specs=[hbm] * 6,
        out_specs=(hbm,) * 6,
        scratch_shapes=[pltpu.VMEM(item.shape, item.dtype) for item in results]
        + [pltpu.SemaphoreType.DMA((6,))] * 2,
        name="store",
        compiler_params=pltpu.CompilerParams(vmem_limit_bytes=GRANT),
    )(*results)
    return (
        mixed[None],
        gq[None],
        gk[None],
        gv[None],
        gres.T,
        gshort,
    )


def solution(mesh):
    placed = P("dp", "ctx", None)
    return jax.shard_map(
        shards,
        mesh=mesh,
        in_specs=(placed, placed, placed, placed, P(), P(), P()),
        out_specs=(placed, placed, placed, placed, P("ctx", None), P()),
        check_vma=False,
    )
```

```python
import functools

import jax
import jax.numpy as jnp
from jax import lax
from jax.experimental import pallas as pl
from jax.experimental.pallas import tpu as pltpu
from jax.sharding import PartitionSpec as P

MESH = pl.DeviceIdType.MESH
ROWS = 128
CHANNELS = 2048
MODES = 8
LANES = 128
BLOCKS = CHANNELS // LANES
WIDE = 256
NZ = 16
NY = 4
NDP = 8
PLANE = NY * NDP
QUARTER = CHANNELS // NY
GRANT = 56 << 20
F32 = jnp.float32
BF16 = jnp.bfloat16


def split_bf16(value):
    high = value.astype(BF16).astype(F32)
    return high, value - high


def two_row_tile(first, second, at):
    width = first.shape[1]
    row = lax.broadcasted_iota(jnp.int32, (8, width), 0)
    return jnp.where(row == at, first, jnp.where(row == at + 1, second, 0.0))


def rate_rows(rate_ref, width):
    row = lax.broadcasted_iota(jnp.int32, (MODES, width), 0)
    total = jnp.zeros((MODES, width), F32)
    for mode in range(MODES):
        total = jnp.where(row == mode, rate_ref[mode], total)
    return total


def farthest_first(index):
    half = (index + 1) // 2
    return NZ // 2 + half * (1 - 2 * lax.rem(index, 2))


PLANE_STEPS = [
    (dy, dx, core)
    for dy, dx, core in sorted(
        ((dy, dx, core) for dy in range(NY) for dx in range(NDP // 2) for core in range(2)),
        key=lambda at: (-min(at[0], NY - at[0]) - min(at[1], NDP // 2 - at[1]), at),
    )
    if (dy, dx, core) != (0, 0, 0)
]


def operator_kernel(
    rate_ref,
    q_hbm,
    k_hbm,
    v_hbm,
    go_hbm,
    filter_ref,
    residue_ref,
    mixed_hbm,
    gq_hbm,
    gk_hbm,
    gv_hbm,
    gres_ref,
    gshort_ref,
    mixed_ref,
    gq_ref,
    gk_ref,
    gv_ref,
    q_ref,
    k_ref,
    v_ref,
    go_ref,
    tail_send,
    head_send,
    tail_recv,
    head_recv,
    short_q,
    short_k,
    short_v,
    gated,
    d_conv,
    tail_gd,
    fwd_table,
    bwd_table,
    modal,
    conv_local,
    back_local,
    res_local,
    ends,
    y_send,
    y_recv,
    z_send,
    z_recv,
    b_send,
    b_recv,
    enter,
    edge,
    e_send,
    e_recv,
    e_prev,
    m_send,
    m_recv,
    l_send,
    l_recv,
    r_send,
    r_recv,
    p_send,
    p_recv,
    short_sum,
    res_sum,
    load_sems,
    store_sems,
    send_sems,
    recv_sems,
):
    ctx = lax.axis_index("ctx")
    dp = lax.axis_index("dp")
    z = ctx // NY
    y = lax.rem(ctx, NY)

    inputs = (q_ref, k_ref, v_ref, go_ref)
    loads = [
        pltpu.make_async_copy(source, target, load_sems.at[index])
        for index, (source, target) in enumerate(zip((q_hbm, k_hbm, v_hbm, go_hbm), inputs))
    ]
    for load in loads:
        load.start()

    barrier = pltpu.get_barrier_semaphore()
    count = NZ * NY
    following = lax.rem(ctx + 1, count)
    preceding = lax.rem(ctx + count - 1, count)
    column = dp // 2
    core = lax.rem(dp, 2)

    def line_peer(index):
        return lax.rem(z + farthest_first(index), NZ)

    def plane_device(step):
        dy, dx, dcore = step
        peer_x = lax.rem(column + dx, NDP // 2)
        peer_core = (1 - core) if dcore else core
        return {"ctx": z * NY + lax.rem(y + dy, NY), "dp": peer_x * 2 + peer_core}

    def greet_line(index, carry):
        pl.semaphore_signal(
            barrier, inc=1, device_id={"ctx": line_peer(index) * NY + y}, device_id_type=MESH
        )
        return carry

    lax.fori_loop(0, NZ - 1, greet_line, 0)
    for step in PLANE_STEPS:
        pl.semaphore_signal(
            barrier, inc=1, device_id=plane_device(step), device_id_type=MESH
        )
    for neighbour in (following, preceding):
        pl.semaphore_signal(
            barrier, inc=1, device_id={"ctx": neighbour}, device_id_type=MESH
        )

    @pl.when(jnp.logical_or(y == 1, y == 2))
    def _():
        sender = lax.rem(z + NZ - 1, NZ) * NY + NY - 1
        pl.semaphore_signal(barrier, inc=1, device_id={"ctx": sender}, device_id_type=MESH)

    def taps(branch, lanes):
        return [filter_ref[branch, j : j + 1, lanes] for j in range(3)]

    row_at = lax.broadcasted_iota(jnp.int32, (ROWS, ROWS), 0)
    col_at = lax.broadcasted_iota(jnp.int32, (ROWS, ROWS), 1)
    for mode in range(MODES):
        speed = rate_ref[mode]
        here = slice(mode * ROWS, (mode + 1) * ROWS)
        for table, lag in ((fwd_table, row_at - col_at), (bwd_table, col_at - row_at)):
            power = jnp.exp(-speed * jnp.maximum(lag, 0).astype(F32))
            high, low = split_bf16(jnp.where(lag >= 0, power, 0.0))
            table[here, 0:ROWS] = high.astype(BF16)
            table[here, ROWS : 2 * ROWS] = low.astype(BF16)

    for load in loads:
        load.wait()

    row_eight = lax.broadcasted_iota(jnp.int32, (8, CHANNELS), 0)
    tails = jnp.zeros((8, CHANNELS), F32)
    heads = jnp.zeros((8, CHANNELS), F32)
    for branch in range(4):
        last = inputs[branch][ROWS - 16 : ROWS, :].astype(F32)
        first = inputs[branch][0:16, :].astype(F32)
        for index in range(2):
            here = row_eight == 2 * branch + index
            heads = jnp.where(here, first[index : index + 1], heads)
            if branch < 3:
                tails = jnp.where(here, last[14 + index : 15 + index], tails)
    tail_send[...] = tails.astype(BF16)
    head_send[...] = heads.astype(BF16)
    edges = jnp.concatenate([tails, heads], axis=0).astype(BF16)
    for part in range(NY):
        e_send[part] = edges[:, part * QUARTER : (part + 1) * QUARTER]

    def before_tile(branch, lanes):
        rows = tail_recv[:, lanes].astype(F32)[2 * branch : 2 * branch + 2]
        tile = two_row_tile(rows[0:1], rows[1:2], 6)
        return jnp.where(ctx == 0, 0.0, tile)

    def after_tile(branch, lanes):
        rows = head_recv[:, lanes].astype(F32)[2 * branch : 2 * branch + 2]
        tile = two_row_tile(rows[0:1], rows[1:2], 0)
        return jnp.where(ctx == count - 1, 0.0, tile)

    shorts = (short_q, short_k, short_v)

    def convolve(branch, lanes, extended):
        first, second, third = taps(branch, lanes)
        return (
            first * extended[8:]
            + second * pltpu.roll(extended, 1, 0)[8:]
            + third * pltpu.roll(extended, 2, 0)[8:]
        )

    def short_step(block, carry):
        lanes = pl.ds(pl.multiple_of(block * LANES, LANES), LANES)
        results = []
        for branch in range(3):
            values = inputs[branch][:, lanes].astype(F32)
            extended = jnp.concatenate([jnp.zeros((8, LANES), F32), values], axis=0)
            total = convolve(branch, lanes, extended)
            shorts[branch][0:ROWS, lanes] = total
            results.append(total)
        query, keyed, valued = results
        gated[:, lanes] = (keyed * valued).astype(BF16)
        d_conv[:, lanes] = (go_ref[:, lanes].astype(F32) * query).astype(BF16)
        return carry

    lax.fori_loop(0, BLOCKS, short_step, 0)

    rates = rate_rows(rate_ref, ROWS)
    place = lax.broadcasted_iota(jnp.int32, (MODES, ROWS), 1).astype(F32)
    def compute_ends():
        for slot, offsets, operand in ((0, ROWS - 1.0 - place, gated), (1, place, d_conv)):
            high, low = split_bf16(jnp.exp(-rates * offsets))
            table = jnp.concatenate([high, low], axis=0).astype(BF16)
            product = jnp.dot(table, operand[...], preferred_element_type=F32)
            ends[slot * 8 : slot * 8 + 8, :] = product[:8] + product[8:]

    compute_ends()

    for part in range(NY):
        y_send[part] = ends[:, part * QUARTER : (part + 1) * QUARTER]

    pl.semaphore_wait(barrier, NZ - 1 + PLANE - 1 + 2 + 2 * (y // (NY - 1)))

    def y_copy(source, target, step, slot):
        peer = lax.rem(y + step, NY)
        return pltpu.make_async_remote_copy(
            src_ref=source.at[peer],
            dst_ref=target.at[y],
            send_sem=send_sems.at[slot],
            recv_sem=recv_sems.at[slot],
            device_id={"ctx": z * NY + peer},
            device_id_type=MESH,
        )

    leaving = []

    def settle(target, number, slot):
        done = pltpu.make_async_remote_copy(
            src_ref=target.at[pl.ds(0, number)],
            dst_ref=target.at[pl.ds(0, number)],
            send_sem=send_sems.at[slot],
            recv_sem=recv_sems.at[slot],
            device_id={"ctx": z * NY + lax.rem(y + 1, NY)},
            device_id_type=MESH,
        )
        done.wait_recv()
        leaving.append(done)

    for step in range(1, NY):
        y_copy(y_send, y_recv, step, 0).start()
    y_recv[y] = y_send[y]
    for step in range(1, NY):
        y_copy(e_send, e_recv, step, 11).start()
    e_recv[y] = e_send[y]

    def onward_copy(part):
        return pltpu.make_async_remote_copy(
            src_ref=e_send.at[part],
            dst_ref=e_prev,
            send_sem=send_sems.at[12],
            recv_sem=recv_sems.at[12],
            device_id={"ctx": lax.rem(z + 1, NZ) * NY + part},
            device_id_type=MESH,
        )

    @pl.when(y == NY - 1)
    def _():
        for part in range(NY):
            onward_copy(part).start()

    halos = [
        pltpu.make_async_remote_copy(
            src_ref=source,
            dst_ref=target,
            send_sem=send_sems.at[slot],
            recv_sem=recv_sems.at[slot],
            device_id={"ctx": neighbour},
            device_id_type=MESH,
        )
        for slot, source, target, neighbour in (
            (6, tail_send, tail_recv, following),
            (7, head_send, head_recv, preceding),
        )
    ]
    for halo in halos:
        halo.start()

    gain_rows = jnp.sqrt(1.0 - jnp.exp(-2.0 * rate_rows(rate_ref, WIDE)))

    def back_step(block, carry):
        lanes = pl.ds(pl.multiple_of(block * WIDE, WIDE), WIDE)
        columns = residue_ref[:, lanes] * gain_rows
        source = d_conv[:, lanes]
        modal[...] = jnp.dot(
            bwd_table[...],
            jnp.concatenate([source, source], axis=0),
            preferred_element_type=F32,
        )
        total = jnp.zeros((ROWS, WIDE), F32)
        for mode in range(MODES):
            total = total + columns[mode : mode + 1] * modal[mode * ROWS : (mode + 1) * ROWS, :]
        back_local[:, lanes] = total
        return carry

    lax.fori_loop(0, CHANNELS // WIDE, back_step, 0)

    settle(y_recv, NY - 1, 0)

    speeds = rate_rows(rate_ref, QUARTER)
    settle(e_recv, NY - 1, 11)
    onward_copy(0).wait_recv()

    mine = pl.ds(pl.multiple_of(y * QUARTER, QUARTER), QUARTER)
    own_taps = [taps(branch, mine) for branch in range(3)]

    def rounded(value):
        return value.astype(BF16).astype(F32)

    for index in range(NY):
        here = e_recv[index].astype(F32)[8:16]
        prior = (e_recv[index - 1] if index else e_prev[...]).astype(F32)[0:8]
        if index == 0:
            prior = jnp.where(z == 0, 0.0, prior)
        plain = []
        full = []
        for branch in range(3):
            first, second, third = own_taps[branch]
            row0, row1 = (here[2 * branch + at : 2 * branch + at + 1] for at in range(2))
            old0, old1 = (prior[2 * branch + at : 2 * branch + at + 1] for at in range(2))
            plain.append((first * row0, first * row1 + second * row0))
            full.append(
                (
                    first * row0 + second * old1 + third * old0,
                    first * row1 + second * row0 + third * old1,
                )
            )
        d_gate = []
        d_out = []
        for at in range(2):
            cot = here[6 + at : 7 + at]
            d_gate.append(
                rounded(full[1][at] * full[2][at]) - rounded(plain[1][at] * plain[2][at])
            )
            d_out.append(rounded(cot * full[0][at]) - rounded(cot * plain[0][at]))
        y_recv[index, 0:8] = (
            y_recv[index, 0:8]
            + jnp.exp(-speeds * (ROWS - 1.0)) * d_gate[0]
            + jnp.exp(-speeds * (ROWS - 2.0)) * d_gate[1]
        )
        y_recv[index, 8:16] = y_recv[index, 8:16] + d_out[0] + jnp.exp(-speeds) * d_out[1]

    step_decay = jnp.exp(-speeds * float(ROWS))
    group_decay = jnp.exp(-speeds * float(ROWS * NY))

    def fold(value):
        return jnp.concatenate([value[:, : QUARTER // 2], value[:, QUARTER // 2 :]], axis=0)

    def unfold(value):
        return jnp.concatenate([value[:8], value[8:]], axis=1)

    ahead_total = y_recv[0, 0:8]
    back_total = y_recv[NY - 1, 8:16]
    for index in range(1, NY):
        ahead_total = ahead_total * step_decay + y_recv[index, 0:8]
        back_total = back_total * step_decay + y_recv[NY - 1 - index, 8:16]
    z_send[0] = fold(ahead_total).astype(BF16)
    z_send[1] = fold(back_total).astype(BF16)

    def z_start(index, carry):
        peer = line_peer(index)
        pltpu.make_async_remote_copy(
            src_ref=z_send.at[jnp.where(peer < z, 1, 0)],
            dst_ref=z_recv.at[z],
            send_sem=send_sems.at[1],
            recv_sem=recv_sems.at[1],
            device_id={"ctx": peer * NY + y},
            device_id_type=MESH,
        ).start()
        return carry

    lax.fori_loop(0, NZ - 1, z_start, 0)
    z_recv[z] = jnp.zeros((16, QUARTER // 2), BF16)
    for halo in halos:
        halo.wait_recv()

    def patch_step(block, carry):
        lanes = pl.ds(pl.multiple_of(block * LANES, LANES), LANES)
        firsts = []
        nexts = []
        for branch in range(3):
            values = inputs[branch][0:16, lanes].astype(F32)
            extended = jnp.concatenate([before_tile(branch, lanes), values], axis=0)
            firsts.append(convolve(branch, lanes, extended))
            shorts[branch][0:16, lanes] = firsts[branch]
            values = inputs[branch][ROWS - 16 : ROWS, lanes].astype(F32)[8:]
            extended = jnp.concatenate([values, after_tile(branch, lanes)], axis=0)
            nexts.append(convolve(branch, lanes, extended))
            shorts[branch][ROWS : ROWS + 8, lanes] = nexts[branch]
        gated[0:16, lanes] = (firsts[1] * firsts[2]).astype(BF16)
        fresh = (go_ref[0:16, lanes].astype(F32) * firsts[0]).astype(BF16)
        change = fresh.astype(F32) - d_conv[0:16, lanes].astype(F32)
        d_conv[0:16, lanes] = fresh
        columns = residue_ref[:, lanes] * gain_rows[:, :LANES]
        whole = jnp.sum(columns, axis=0, keepdims=True)
        decayed = jnp.sum(columns * jnp.exp(-rates), axis=0, keepdims=True)
        back_local[0:8, lanes] = back_local[0:8, lanes] + two_row_tile(
            whole * change[0:1] + decayed * change[1:2], whole * change[1:2], 0
        )
        tail_gd[0:8, lanes] = (nexts[1] * nexts[2]).astype(BF16).astype(F32)
        tail_gd[8:16, lanes] = (after_tile(3, lanes) * nexts[0]).astype(BF16).astype(F32)
        return carry

    lax.fori_loop(0, BLOCKS, patch_step, 0)

    compute_ends()

    place = lax.broadcasted_iota(jnp.int32, (MODES, ROWS), 1).astype(F32)
    weigh_fwd = jnp.exp(-rates * (place + 1.0)).astype(BF16)
    weigh_back = jnp.exp(-rates * (ROWS - place)).astype(BF16)

    def partner(branch, lanes):
        if branch == 0:
            return go_ref[:, lanes].astype(F32)
        return (short_v if branch == 1 else short_k)[0:ROWS, lanes]

    def moved_rows(branch, lanes):
        extended = jnp.concatenate(
            [before_tile(branch, lanes), inputs[branch][:, lanes].astype(F32)], axis=0
        )
        return [extended[8:]] + [pltpu.roll(extended, tap_at, 0)[8:] for tap_at in (1, 2)]

    def moment_step(block, carry):
        lanes = pl.ds(pl.multiple_of(block * WIDE, WIDE), WIDE)
        part = block // (QUARTER // WIDE)
        inner = pl.ds(pl.multiple_of(lax.rem(block, QUARTER // WIDE) * WIDE, WIDE), WIDE)
        for branch in range(3):
            weigh = weigh_back if branch else weigh_fwd
            other = partner(branch, lanes)
            for tap_at, moved in enumerate(moved_rows(branch, lanes)):
                product = jnp.dot(
                    weigh, (other * moved).astype(BF16), preferred_element_type=F32
                )
                m_send[part, branch * 3 + tap_at, :, inner] = product.astype(BF16)
        return carry

    lax.fori_loop(0, CHANNELS // WIDE, moment_step, 0)

    for step in range(1, NY):
        y_copy(m_send, m_recv, step, 8).start()
    m_recv[y] = m_send[y]

    def modal_step(block, carry):
        lanes = pl.ds(pl.multiple_of(block * WIDE, WIDE), WIDE)
        columns = residue_ref[:, lanes] * gain_rows
        source = gated[:, lanes]
        modal[...] = jnp.dot(
            fwd_table[...],
            jnp.concatenate([source, source], axis=0),
            preferred_element_type=F32,
        )
        cot = d_conv[:, lanes].astype(F32)
        total = jnp.zeros((ROWS, WIDE), F32)
        for mode in range(MODES):
            state = modal[mode * ROWS : (mode + 1) * ROWS, :]
            total = total + columns[mode : mode + 1] * state
            res_local[mode : mode + 1, lanes] = jnp.sum(cot * state, axis=0, keepdims=True)
        conv_local[:, lanes] = total
        return carry

    lax.fori_loop(0, CHANNELS // WIDE, modal_step, 0)

    def local_step(block, carry):
        lanes = pl.ds(pl.multiple_of(block * LANES, LANES), LANES)
        for branch in range(3):
            filtered = (back_local if branch else conv_local)[:, lanes]
            value = filtered * partner(branch, lanes)
            for tap_at, moved in enumerate(moved_rows(branch, lanes)):
                at = branch * 3 + tap_at
                l_send[2 * block, at : at + 1] = jnp.sum(value * moved, axis=0, keepdims=True)
        l_send[2 * block + 1, 0:8] = res_local[:, lanes] * gain_rows[:, :LANES]
        l_send[2 * block + 1, 8:9] = jnp.zeros((1, LANES), F32)
        return carry

    lax.fori_loop(0, BLOCKS, local_step, 0)

    plane = y * NDP + dp
    for step in PLANE_STEPS:
        where = plane_device(step)
        piece = lax.rem(y + step[0], NY) * NDP + where["dp"]
        pltpu.make_async_remote_copy(
            src_ref=l_send.at[piece],
            dst_ref=l_recv.at[plane],
            send_sem=send_sems.at[9],
            recv_sem=recv_sems.at[9],
            device_id=where,
            device_id_type=MESH,
        ).start()
    l_recv[plane] = l_send[plane]

    settle(z_recv, NZ - 1, 1)

    start = jnp.zeros((MODES, QUARTER), F32)
    finish = jnp.zeros((MODES, QUARTER), F32)
    for index in range(NZ):
        start = jnp.where(
            index < z, start * group_decay + unfold(z_recv[index].astype(F32)), start
        )
        other = NZ - 1 - index
        finish = jnp.where(
            other > z, finish * group_decay + unfold(z_recv[other].astype(F32)), finish
        )
    for index in range(NY):
        b_send[index, 0:8] = start
        start = start * step_decay + y_recv[index, 0:8]
        other = NY - 1 - index
        b_send[other, 8:16] = finish
        finish = finish * step_decay + y_recv[other, 8:16]

    one = jnp.exp(-speeds)
    gains = jnp.sqrt(1.0 - jnp.exp(-2.0 * speeds))
    own_columns = residue_ref[:, mine] * gains
    settle(m_recv, NY - 1, 8)
    pairs = jnp.zeros((MODES, QUARTER), F32)
    for index in range(NY):
        pairs = pairs + b_send[index, 0:8] * y_recv[index, 8:16]
    res_part = gains * one * pairs
    for branch in range(3):
        half = slice(8, 16) if branch else slice(0, 8)
        for tap_at in range(3):
            at = branch * 3 + tap_at
            pairs = jnp.zeros((MODES, QUARTER), F32)
            for index in range(NY):
                pairs = pairs + b_send[index, half] * m_recv[index, at].astype(F32)
            row = jnp.sum(own_columns * pairs, axis=0, keepdims=True)
            for offset in range(NDP // 2):
                r_send[2 * offset, at : at + 1] = row[:, offset * LANES : (offset + 1) * LANES]
    for offset in range(NDP // 2):
        r_send[2 * offset + 1, 0:8] = res_part[:, offset * LANES : (offset + 1) * LANES]
        r_send[2 * offset + 1, 8:9] = jnp.zeros((1, LANES), F32)

    for step in range(1, NDP):
        peer = lax.rem(dp + step, NDP)
        pltpu.make_async_remote_copy(
            src_ref=r_send.at[peer],
            dst_ref=r_recv.at[dp],
            send_sem=send_sems.at[3],
            recv_sem=recv_sems.at[3],
            device_id={"dp": peer},
            device_id_type=MESH,
        ).start()
    for step in range(1, NY):
        y_copy(b_send, b_recv, step, 2).start()
    b_recv[y] = b_send[y]

    r_recv[dp] = r_send[dp]
    settle(l_recv, PLANE - 1, 9)
    total = l_recv[0]
    for index in range(1, PLANE):
        total = total + l_recv[index]
    settle(r_recv, NDP - 1, 3)
    for index in range(NDP):
        total = total + r_recv[index]
    p_send[...] = total
    p_recv[z] = total

    block_here = y * (NDP // 2) + column
    res_home = jnp.logical_and(core == 1, block_here == z)

    def line_copy(peer):
        return pltpu.make_async_remote_copy(
            src_ref=p_send,
            dst_ref=p_recv.at[z],
            send_sem=send_sems.at[4],
            recv_sem=recv_sems.at[4],
            device_id={"ctx": peer * NY + y},
            device_id_type=MESH,
        )

    @pl.when(core == 0)
    def _():
        def line_start(index, carry):
            line_copy(line_peer(index)).start()
            return carry

        lax.fori_loop(0, NZ - 1, line_start, 0)

    @pl.when(jnp.logical_and(core == 1, block_here != z))
    def _():
        line_copy(block_here).start()

    settle(b_recv, NY - 1, 2)

    for part in range(NY):
        lanes = slice(part * QUARTER, (part + 1) * QUARTER)
        columns = residue_ref[:, lanes] * gains
        state = b_recv[part, 0:8]
        costate = b_recv[part, 8:16]
        for slot, value in ((0, columns * state), (1, columns * costate)):
            high, low = split_bf16(value)
            enter[slot, :, lanes] = jnp.concatenate([high, low, high, low], axis=0).astype(BF16)
        out_state = state * step_decay + ends[0:8, lanes]
        next_first = one * out_state + tail_gd[0:1, lanes]
        next_second = one * next_first + tail_gd[1:2, lanes]
        back_second = (costate - tail_gd[8:9, lanes]) / one
        edge[0:8, lanes] = two_row_tile(
            jnp.sum(columns * next_first, axis=0, keepdims=True),
            jnp.sum(columns * next_second, axis=0, keepdims=True),
            0,
        )
        edge[8:16, lanes] = two_row_tile(
            jnp.sum(columns * costate, axis=0, keepdims=True),
            jnp.sum(columns * back_second, axis=0, keepdims=True),
            0,
        )

    lane_at = lax.broadcasted_iota(jnp.int32, (ROWS, 4 * MODES), 1)
    lane_rate = jnp.zeros((ROWS, 4 * MODES), F32)
    for mode in range(MODES):
        lane_rate = jnp.where(lax.rem(lane_at, MODES) == mode, rate_ref[mode], lane_rate)
    place = lax.broadcasted_iota(jnp.int32, (ROWS, 4 * MODES), 0).astype(F32)

    def spread(offsets):
        high, low = split_bf16(jnp.exp(-lane_rate * offsets))
        return jnp.where(lane_at < 2 * MODES, high, low).astype(BF16)

    spread_fwd = spread(place + 1.0)
    spread_back = spread(ROWS - place)
    outs = (gq_ref, gk_ref, gv_ref)

    def final_step(block, carry):
        lanes = pl.ds(pl.multiple_of(block * LANES, LANES), LANES)
        conv = conv_local[:, lanes] + jnp.dot(
            spread_fwd, enter[0, :, lanes], preferred_element_type=F32
        )
        back = back_local[:, lanes] + jnp.dot(
            spread_back, enter[1, :, lanes], preferred_element_type=F32
        )
        conv_ext = jnp.concatenate([conv, edge[0:8, lanes]], axis=0)
        back_ext = jnp.concatenate([back, edge[8:16, lanes]], axis=0)
        cot = jnp.concatenate([go_ref[:, lanes].astype(F32), after_tile(3, lanes)], axis=0)
        mixed_ref[:, lanes] = (short_q[0:ROWS, lanes] * conv).astype(BF16)
        d_shorts = (cot * conv_ext, back_ext * short_v[:, lanes], back_ext * short_k[:, lanes])
        for branch in range(3):
            value = d_shorts[branch]
            first, second, third = taps(branch, lanes)
            total = (
                first * value[:ROWS]
                + second * pltpu.roll(value, ROWS + 8 - 1, 0)[:ROWS]
                + third * pltpu.roll(value, ROWS + 8 - 2, 0)[:ROWS]
            )
            outs[branch][:, lanes] = total.astype(BF16)
        return carry

    lax.fori_loop(0, BLOCKS, final_step, 0)
    stores = [
        pltpu.make_async_copy(source, target, store_sems.at[index])
        for index, (source, target) in enumerate(
            ((mixed_ref, mixed_hbm), (gq_ref, gq_hbm), (gk_ref, gk_hbm), (gv_ref, gv_hbm))
        )
    ]
    for store in stores:
        store.start()

    def await_line():
        done = pltpu.make_async_remote_copy(
            src_ref=p_recv.at[pl.ds(0, NZ - 1)],
            dst_ref=p_recv.at[pl.ds(0, NZ - 1)],
            send_sem=send_sems.at[4],
            recv_sem=recv_sems.at[4],
            device_id={"ctx": lax.rem(z + 1, NZ) * NY + y},
            device_id_type=MESH,
        )
        done.wait_recv()
        total = p_recv[0]
        for index in range(1, NZ):
            total = total + p_recv[index]
        return total

    def share_copy(source, target, slot, step):
        return pltpu.make_async_remote_copy(
            src_ref=source,
            dst_ref=target,
            send_sem=send_sems.at[slot],
            recv_sem=recv_sems.at[slot],
            device_id=plane_device(step),
            device_id_type=MESH,
        )

    def share(source, target, slot):
        for step in PLANE_STEPS:
            share_copy(source, target, slot, step).start()

    @pl.when(core == 0)
    def _():
        short_sum[block_here] = await_line()
        share(short_sum.at[block_here], short_sum.at[block_here], 5)

    @pl.when(res_home)
    def _():
        res_sum[...] = await_line()
        share(res_sum, res_sum, 10)

    def await_short(number):
        here = short_sum.at[pl.ds(0, number)]
        share_copy(here, here, 5, PLANE_STEPS[0]).wait_recv()

    @pl.when(core == 0)
    def _():
        await_short(BLOCKS - 1)

    @pl.when(core == 1)
    def _():
        await_short(BLOCKS)

    @pl.when(jnp.logical_not(res_home))
    def _():
        share_copy(res_sum, res_sum, 10, PLANE_STEPS[0]).wait_recv()

    for block in range(BLOCKS):
        lanes = slice(block * LANES, (block + 1) * LANES)
        for branch in range(3):
            gshort_ref[branch, :, lanes] = short_sum[block, 3 * branch : 3 * branch + 3]
    gres_ref[...] = pltpu.roll(res_sum[0:8], lax.rem(LANES - 32 * y, LANES), 1)[:, :32]
    for store in stores:
        store.wait()
    for copy in halos + leaving:
        copy.wait_send()

    @pl.when(y == NY - 1)
    def _():
        for part in range(NY):
            onward_copy(part).wait_send()

    @pl.when(core == 0)
    def _():
        here = p_recv.at[pl.ds(0, NZ - 1)]
        pltpu.make_async_remote_copy(
            src_ref=here,
            dst_ref=here,
            send_sem=send_sems.at[4],
            recv_sem=recv_sems.at[4],
            device_id={"ctx": line_peer(0) * NY + y},
            device_id_type=MESH,
        ).wait_send()
        for step in PLANE_STEPS:
            share_copy(short_sum.at[block_here], short_sum.at[block_here], 5, step).wait_send()

    @pl.when(jnp.logical_and(core == 1, block_here != z))
    def _():
        line_copy(block_here).wait_send()

    @pl.when(res_home)
    def _():
        for step in PLANE_STEPS:
            share_copy(res_sum, res_sum, 10, step).wait_send()


def store_kernel(*refs):
    sources, targets, stages = refs[:6], refs[6:12], refs[12:18]
    load_sems, store_sems = refs[18:]
    pieces = []
    for source, target, stage in zip(sources, targets, stages):
        rows = source.shape[0]
        for first in range(0, source.shape[0], rows):
            here = pl.ds(first, rows)
            pieces.append((source.at[here], stage.at[here], target.at[here], len(pieces)))
    loads = [
        pltpu.make_async_copy(source, stage, load_sems.at[at]) for source, stage, _, at in pieces
    ]
    stores = [
        pltpu.make_async_copy(stage, target, store_sems.at[at]) for _, stage, target, at in pieces
    ]
    for load in loads:
        load.start()
    for load, store in zip(loads, stores):
        load.wait()
        store.start()
    for store in stores:
        store.wait()


def shards(q_in, k_in, v_in, grad_out, short_filter, residue, rate):
    inputs = (q_in[0], k_in[0], v_in[0], grad_out[0])
    vmem = pl.BlockSpec(memory_space=pltpu.VMEM)
    smem = pl.BlockSpec(memory_space=pltpu.SMEM)
    hbm = pl.BlockSpec(memory_space=pltpu.HBM)
    block = jax.ShapeDtypeStruct((ROWS, CHANNELS), BF16)
    results = pl.pallas_call(
        operator_kernel,
        out_shape=(
            block,
            block,
            block,
            block,
            jax.ShapeDtypeStruct((MODES, 32), F32),
            jax.ShapeDtypeStruct((3, 3, CHANNELS), F32),
        ),
        in_specs=[smem] + [hbm] * 4 + [vmem] * 2,
        out_specs=(hbm,) * 4 + (vmem,) * 2,
        scratch_shapes=[pltpu.VMEM((ROWS, CHANNELS), BF16)] * 8
        + [pltpu.VMEM((8, CHANNELS), BF16)] * 4
        + [
            pltpu.VMEM((ROWS + 8, CHANNELS), F32),
            pltpu.VMEM((ROWS + 8, CHANNELS), F32),
            pltpu.VMEM((ROWS + 8, CHANNELS), F32),
            pltpu.VMEM((ROWS, CHANNELS), BF16),
            pltpu.VMEM((ROWS, CHANNELS), BF16),
            pltpu.VMEM((16, CHANNELS), F32),
            pltpu.VMEM((MODES * ROWS, 2 * ROWS), BF16),
            pltpu.VMEM((MODES * ROWS, 2 * ROWS), BF16),
            pltpu.VMEM((MODES * ROWS, WIDE), F32),
            pltpu.VMEM((ROWS, CHANNELS), F32),
            pltpu.VMEM((ROWS, CHANNELS), F32),
            pltpu.VMEM((MODES, CHANNELS), F32),
            pltpu.VMEM((16, CHANNELS), F32),
            pltpu.VMEM((NY, 16, QUARTER), F32),
            pltpu.VMEM((NY, 16, QUARTER), F32),
            pltpu.VMEM((2, 16, QUARTER // 2), BF16),
            pltpu.VMEM((NZ, 16, QUARTER // 2), BF16),
            pltpu.VMEM((NY, 16, QUARTER), F32),
            pltpu.VMEM((NY, 16, QUARTER), F32),
            pltpu.VMEM((2, 4 * MODES, CHANNELS), BF16),
            pltpu.VMEM((16, CHANNELS), F32),
            pltpu.VMEM((NY, 16, QUARTER), BF16),
            pltpu.VMEM((NY, 16, QUARTER), BF16),
            pltpu.VMEM((16, QUARTER), BF16),
            pltpu.VMEM((NY, 9, MODES, QUARTER), BF16),
            pltpu.VMEM((NY, 9, MODES, QUARTER), BF16),
            pltpu.VMEM((PLANE, 9, LANES), F32),
            pltpu.VMEM((PLANE, 9, LANES), F32),
            pltpu.VMEM((NDP, 9, LANES), F32),
            pltpu.VMEM((NDP, 9, LANES), F32),
            pltpu.VMEM((9, LANES), F32),
            pltpu.VMEM((NZ, 9, LANES), F32),
            pltpu.VMEM((BLOCKS, 9, LANES), F32),
            pltpu.VMEM((9, LANES), F32),
            pltpu.SemaphoreType.DMA((4,)),
            pltpu.SemaphoreType.DMA((4,)),
            pltpu.SemaphoreType.DMA((13,)),
            pltpu.SemaphoreType.DMA((13,)),
        ],
        name="operator",
        compiler_params=pltpu.CompilerParams(
            collective_id=0, has_side_effects=True, vmem_limit_bytes=GRANT
        ),
    )(rate, *inputs, short_filter, residue.T)
    mixed, gq, gk, gv, gres, gshort = pl.pallas_call(
        store_kernel,
        out_shape=tuple(jax.ShapeDtypeStruct(item.shape, item.dtype) for item in results),
        in_specs=[hbm] * 6,
        out_specs=(hbm,) * 6,
        scratch_shapes=[pltpu.VMEM(item.shape, item.dtype) for item in results]
        + [pltpu.SemaphoreType.DMA((6,))] * 2,
        name="store",
        compiler_params=pltpu.CompilerParams(vmem_limit_bytes=GRANT),
    )(*results)
    return (
        mixed[None],
        gq[None],
        gk[None],
        gv[None],
        gres.T,
        gshort,
    )


def solution(mesh):
    placed = P("dp", "ctx", None)
    return jax.shard_map(
        shards,
        mesh=mesh,
        in_specs=(placed, placed, placed, placed, P(), P(), P()),
        out_specs=(placed, placed, placed, placed, P("ctx", None), P()),
        check_vma=False,
    )
```
